1024 devices in a mesh: stream: 256 (over y, z, core), span: 4 (over x).
Axes of the slice: x: 4, y: 8, z: 16, core: 2. Of those that a mesh axis runs over, the one named last changes fastest.
Arguments:
- basis: float32 [4, 10, 2048, 8, 512], P(None, None, 'stream', None, 'span'), may hold values from -6 to 6
- coeffs: float32 [4], replicated, may hold values from -3 to 3
- mixing_matrix: float32 [10, 10], replicated, may hold values from -2 to 2
- base_speed: float32 [2048, 8, 512], P('stream', None, 'span'), may hold values from 0.5 to 1.5
- span_speed: float32 [2048, 8, 512], P('stream', None, 'span'), may hold values from -2.4 to 2.4
- polymer_gain: float32 [2048, 8, 512], P('stream', None, 'span'), may hold values from 0.3 to 3
Outputs:
- proj: float32 [4, 4], replicated
- rfactor: float32 [4, 4], replicated
- basis_new: float32 [4, 10, 2048, 8, 512], P(None, None, 'stream', None, 'span')
The draws below stay inside these ranges and needn't reach their ends.
All inputs are finite; a program needn't handle non-finite values.
Results may differ from the reference program's by a relative error of at most 0.00025.
Values sent between devices are 32-bit elements; how exact they have to be, the bound alone decides.
No kernel may reach another device: no remote copies, remote signals or barrier semaphores. Data moves between devices by JAX's collectives and lax.ppermute only.
A program may use at most 32 MiB of HBM per device.

```python
import math
import jax
import jax.numpy as jnp
from jax import lax

F = 10
NY = 8
M = 4
STEPS = 4
NX = 2048
NZ = 512
NTOT = 83886080


def shard_levels(own_key, shape, split, least, high):
    gain = 1.0
    for dim, parts in split:
        steps = jax.random.uniform(jax.random.fold_in(jax.random.fold_in(own_key, 6), dim), (parts,), jnp.float32, least / len(split), high / len(split))
        gain = gain * jnp.repeat(jnp.exp(steps), shape[dim] // parts).reshape((-1,) + (1,) * (len(shape) - 1 - dim))
    return gain


def noise(key, dims, width, bound, pieces=(), held_as=jnp.bfloat16):
    values = jax.random.normal(key, dims, jnp.float32) * width
    if len(pieces) > 0:
        values = shard_levels(key, dims, pieces, -0.22, 0.18) * values
    return jnp.clip(values, min=-bound, max=bound).astype(held_as)


def setup_inputs(seed: int = 0) -> dict:
    key_list = jax.random.split(jax.random.key(seed), 7)
    basis = noise(key_list[0], (M, F, NX, NY, NZ), 1.0, 6.0, ((2, 256), (4, 4)), jnp.float32)
    coeffs = noise(key_list[1], (M,), 0.5, 3.0, (), jnp.float32)
    mixing_matrix = noise(key_list[2], (F, F), F ** -0.5, 2.0, (), jnp.float32)
    base_speed = jnp.clip(0.5 + 1.0 * jax.random.uniform(key_list[3], (NX, NY, NZ), jnp.float32) ** shard_levels(key_list[3], (NX, NY, NZ), ((0, 256), (2, 4)), -0.2, 0.2), 0.5, 1.5)
    span_speed = noise(key_list[4], (NX, NY, NZ), 0.4, 2.4, ((0, 256), (2, 4)), jnp.float32)
    polymer_gain = jnp.clip(jnp.exp(math.log(3.0) - 2.3025851 * jax.random.uniform(key_list[5], (NX, NY, NZ), jnp.float32) ** shard_levels(key_list[5], (NX, NY, NZ), ((0, 256), (2, 4)), -0.2, 0.2)), 0.3, 3.0)
    return {"basis": basis, "coeffs": coeffs, "mixing_matrix": mixing_matrix, "base_speed": base_speed, "span_speed": span_speed, "polymer_gain": polymer_gain}


def advance(values_now, base_speed, span_speed, polymer_gain, mixing_matrix):
    center_part = values_now[:, 1:-1, :, 1:-1]
    forward_x = values_now[:, 2:, :, 1:-1]
    backward_x = values_now[:, :-2, :, 1:-1]
    forward_z = values_now[:, 1:-1, :, 2:]
    backward_z = values_now[:, 1:-1, :, :-2]
    zero_row = jnp.zeros_like(center_part[:, :, :1, :])
    wall_up = jnp.concatenate([center_part[:, :, 1:, :], zero_row], axis=2)
    wall_down = jnp.concatenate([zero_row, center_part[:, :, :-1, :]], axis=2)
    laplace = forward_x + backward_x + forward_z + backward_z + wall_up + wall_down - 6.0 * center_part
    mixing = jnp.einsum('fg,gxyz->fxyz', mixing_matrix, center_part, precision=lax.Precision.HIGHEST)
    return -base_speed * (forward_x - backward_x) * 0.5 - span_speed * (forward_z - backward_z) * 0.5 + 0.05 * laplace + polymer_gain * mixing

def reference(basis, coeffs, mixing_matrix, base_speed, span_speed, polymer_gain):
    start = jnp.einsum('m,mfxyz->fxyz', coeffs, basis, precision=lax.Precision.HIGHEST)
    current = start
    krylov = []
    for section in range(STEPS):
        padded = jnp.pad(current, ((0, 0), (1, 1), (0, 0), (1, 1)), mode='wrap')
        current = advance(padded, base_speed, span_speed, polymer_gain, mixing_matrix)
        krylov.append(current)
    stacked = jnp.stack(krylov, 0)
    total = float(NTOT)
    flat_basis = basis.reshape(M, -1)
    flat_new = stacked.reshape(STEPS, -1)
    proj = jnp.dot(flat_basis, flat_new.T, precision=lax.Precision.HIGHEST) / total
    projected = flat_new - jnp.dot(proj.T, flat_basis, precision=lax.Precision.HIGHEST)
    gram = jnp.dot(projected, projected.T, precision=lax.Precision.HIGHEST) / total
    lower_factor = jnp.linalg.cholesky(gram)
    solved = jax.scipy.linalg.solve_triangular(lower_factor, projected, lower=True)
    return (proj, lower_factor.T, solved.reshape(stacked.shape))
```

```python
import functools

import jax
import jax.numpy as jnp
import numpy as np
from jax import lax
from jax.experimental import pallas as pl
from jax.experimental.pallas import tpu as pltpu
from jax.sharding import Mesh
from jax.sharding import PartitionSpec as P

STEPS = 4
LANES = 128
EXTRA = 3
VMEM = pl.BlockSpec(memory_space=pltpu.VMEM)
SMEM = pl.BlockSpec(memory_space=pltpu.SMEM)
PAIRS = [(a, b) for a in range(STEPS) for b in range(a, STEPS)]


def lane_index():
    return lax.broadcasted_iota(jnp.int32, (8, LANES), 1)


def row_index():
    return lax.broadcasted_iota(jnp.int32, (8, LANES), 0)


def start_kernel(coeffs, basis, base_speed, span_speed, gain, low, high):
    count, fields = basis.shape[0], basis.shape[1]

    def field(f, carry):
        for x in range(2 * STEPS):
            value = coeffs[0] * basis[0, f, x]
            for m in range(1, count):
                value = value + coeffs[m] * basis[m, f, x]
            (low if x < STEPS else high)[f, x % STEPS] = value
        return carry

    lax.fori_loop(0, fields, field, 0)
    for e, ref in enumerate((base_speed, span_speed, gain)):
        low[fields + e] = ref[:STEPS]
        high[fields + e] = ref[STEPS:]


def edges_kernel(before, low, high, after, packed):
    group = lane_index() // 8

    def field(f, carry):
        value = jnp.zeros((8, LANES), jnp.float32)
        for r in range(4 * STEPS):
            ref = (before, low, high, after)[r // STEPS]
            turned = pltpu.roll(ref[f, r % STEPS], (8 * r + 4) % LANES, 1)
            value = jnp.where(group == r, turned, value)
        packed[f] = value
        return carry

    lax.fori_loop(0, packed.shape[0], field, 0)


def stencil(values, x_up, x_down, z_up, z_down, base, span, gain, mixing, up_wall, down_wall):
    half_x, half_z = 0.5 * base, 0.5 * span
    c_xu, c_xd, c_zu, c_zd = 0.05 - half_x, 0.05 + half_x, 0.05 - half_z, 0.05 + half_z
    out = []
    for f, v in enumerate(values):
        mixed = mixing[f, 0] * values[0]
        for g in range(1, len(values)):
            mixed = mixed + mixing[f, g] * values[g]
        near_x = c_xu * x_up(f) + c_xd * x_down(f)
        near_z = c_zu * z_up(f) + c_zd * z_down(f)
        near_y = up_wall * pltpu.roll(v, 7, 0) + down_wall * pltpu.roll(v, 1, 0)
        out.append((near_x + near_z) + (near_y - 0.3 * v) + gain * mixed)
    return out


def krylov_kernel(
    mixing, before, low, high, after, own, left, right, basis, krylov, sums, state, rim, inject
):
    fields, rows = basis.shape[1], 4 * STEPS
    lane, sub = lane_index(), row_index()
    up_wall = jnp.where(sub < 7, 0.05, 0.0).astype(jnp.float32)
    down_wall = jnp.where(sub > 0, 0.05, 0.0).astype(jnp.float32)
    inner = lane % 8 < 4

    def load(f, carry):
        for q, ref in enumerate((before, low, high, after)):
            for r in range(STEPS):
                state[0, f, q * STEPS + r] = ref[f, r]
        mine = own[f]
        rim[0, f, 0] = jnp.where(inner, left[f], mine)
        rim[0, f, 1] = jnp.where(inner, mine, right[f])
        return carry

    lax.fori_loop(0, fields + EXTRA, load, 0)

    for k in range(STEPS):
        src, dst = state.at[k % 2], state.at[(k + 1) % 2]
        rim_src, rim_dst = rim.at[k % 2], rim.at[(k + 1) % 2]
        for f in range(fields):
            inject[f] = jnp.where(lane % 8 == 5, pltpu.roll(rim_src[f, 0], 2, 1), rim_src[f, 1])
        if k + 1 < STEPS:
            for e in range(2):
                values = [rim_src[f, e] for f in range(fields)]
                made = stencil(
                    values,
                    lambda f: pltpu.roll(values[f], LANES - 8, 1),
                    lambda f: pltpu.roll(values[f], 8, 1),
                    lambda f: pltpu.roll(values[f], LANES - 1, 1),
                    lambda f: pltpu.roll(values[f], 1, 1),
                    rim[0, fields, e],
                    rim[0, fields + 1, e],
                    rim[0, fields + 2, e],
                    mixing,
                    up_wall,
                    down_wall,
                )
                for f in range(fields):
                    rim_dst[f, e] = made[f]

        def row(r, carry):
            values = [src[f, r] for f in range(fields)]
            turned = [pltpu.roll(inject[f], 123 - 8 * r, 1) for f in range(fields)]
            made = stencil(
                values,
                lambda f: src[f, r + 1],
                lambda f: src[f, r - 1],
                lambda f: jnp.where(lane == LANES - 1, turned[f], pltpu.roll(values[f], LANES - 1, 1)),
                lambda f: jnp.where(lane == 0, turned[f], pltpu.roll(values[f], 1, 1)),
                state[0, fields, r],
                state[0, fields + 1, r],
                state[0, fields + 2, r],
                mixing,
                up_wall,
                down_wall,
            )
            for f in range(fields):
                dst[f, r] = made[f]
            return carry

        lax.fori_loop(k + 1, rows - k - 1, row, 0)
        krylov[k] = dst[:fields, STEPS : 3 * STEPS]

    def products(f, totals):
        totals = list(totals)
        for x in range(2 * STEPS):
            new = [krylov[k, f, x] for k in range(STEPS)]
            old = [basis[m, f, x] for m in range(STEPS)]
            i = 0
            for a in range(STEPS):
                for b in range(STEPS):
                    totals[i] = totals[i] + old[a] * new[b]
                    i += 1
            for group in (new, old):
                for a, b in PAIRS:
                    totals[i] = totals[i] + group[a] * group[b]
                    i += 1
        return tuple(totals)

    count = STEPS * STEPS + 2 * len(PAIRS)
    zero = jnp.zeros((8, LANES), jnp.float32)
    totals = lax.fori_loop(0, fields, products, (zero,) * count)
    lines = [jnp.sum(t, axis=0, keepdims=True) for t in totals]
    lines.append(jnp.zeros((LANES - count, LANES), jnp.float32))
    table = jnp.concatenate(lines, axis=0)
    row_sums = lax.dot_general(
        jnp.ones((8, LANES), jnp.float32),
        table,
        (((1,), (1,)), ((), ())),
        precision=lax.Precision.HIGHEST,
        preferred_element_type=jnp.float32,
    )
    for i in range(sums.shape[0]):
        sums[i] = row_sums[0:1]


def finish_kernel(total, parts, krylov, basis, proj_out, factor_out, new_out):
    fields = basis.shape[1]
    line = parts[0]
    for i in range(1, parts.shape[0]):
        line = line + parts[i]
    line = jnp.broadcast_to(line / total, (8, LANES))
    spread = [
        jnp.broadcast_to(line[:, i : i + 1], (8, LANES))
        for i in range(STEPS * STEPS + 2 * len(PAIRS))
    ]
    proj = [[spread[a * STEPS + b] for b in range(STEPS)] for a in range(STEPS)]
    new_new, old_old = {}, {}
    for i, (a, b) in enumerate(PAIRS):
        new_new[a, b] = spread[STEPS * STEPS + i]
        old_old[a, b] = old_old[b, a] = spread[STEPS * STEPS + len(PAIRS) + i]
    turned = [
        [
            sum(old_old[j, i] * proj[i][k] for i in range(STEPS)) - 2.0 * proj[j][k]
            for k in range(STEPS)
        ]
        for j in range(STEPS)
    ]
    gram = {
        (a, b): new_new[a, b] + sum(proj[j][a] * turned[j][b] for j in range(STEPS))
        for a, b in PAIRS
    }
    lower, inverse = {}, []
    for b in range(STEPS):
        for a in range(b, STEPS):
            value = gram[b, a]
            for c in range(b):
                value = value - lower[a, c] * lower[b, c]
            if a == b:
                lower[a, b] = jnp.sqrt(value)
                inverse.append(1.0 / lower[a, b])
            else:
                lower[a, b] = value * inverse[b]
    lane, sub = lane_index(), row_index()
    proj_tile = jnp.zeros((8, LANES), jnp.float32)
    factor_tile = proj_tile
    for a in range(STEPS):
        for b in range(STEPS):
            here = (sub == a) & (lane == b)
            proj_tile = jnp.where(here, proj[a][b], proj_tile)
            if b >= a:
                factor_tile = jnp.where(here, lower[b, a], factor_tile)
    proj_out[...] = proj_tile[:STEPS, :STEPS]
    factor_out[...] = factor_tile[:STEPS, :STEPS]

    def field(f, carry):
        for x in range(2 * STEPS):
            old = [basis[m, f, x] for m in range(STEPS)]
            made = []
            for k in range(STEPS):
                value = krylov[k, f, x]
                for m in range(STEPS):
                    value = value - proj[m][k] * old[m]
                for c in range(k):
                    value = value - lower[k, c] * made[c]
                made.append(value * inverse[k])
                new_out[k, f, x] = made[k]
        return carry

    lax.fori_loop(0, fields, field, 0)


def exchange(value, axes, size):
    up = [(i, (i + 1) % size) for i in range(size)]
    return lambda v: lax.ppermute(v, axes, up), lambda v: lax.ppermute(v, axes, [(j, i) for i, j in up])


def shape_of(*dims):
    return jax.ShapeDtypeStruct(dims, jnp.float32)


def kept(*dims):
    return pltpu.VMEM(dims, jnp.float32)


def near(*arrays):
    return [pltpu.with_memory_space_constraint(a, pltpu.VMEM) for a in arrays]


def on_device(sizes, basis, coeffs, mixing_matrix, base_speed, span_speed, polymer_gain):
    outer, inner, span = sizes
    count, fields, nx, ny, nz = basis.shape
    total = float(basis[0].size * outer * inner * span)
    everything = fields + EXTRA
    slab = kept(everything, STEPS, ny, nz)
    low, high = pl.pallas_call(
        start_kernel,
        out_shape=(slab, slab),
        in_specs=[SMEM, VMEM, VMEM, VMEM, VMEM],
        out_specs=(VMEM, VMEM),
        compiler_params=pltpu.CompilerParams(vmem_limit_bytes=16 * 2**20),
        name="start",
    )(coeffs, *near(basis, base_speed, span_speed, polymer_gain))
    up, down = exchange(low, ("outer", "inner"), outer * inner)
    before, after = up(high), down(low)
    packed = pl.pallas_call(
        edges_kernel,
        out_shape=kept(everything, ny, nz),
        in_specs=[VMEM] * 4,
        out_specs=VMEM,
        compiler_params=pltpu.CompilerParams(vmem_limit_bytes=16 * 2**20),
        name="edges",
    )(*near(before, low, high, after))
    up, down = exchange(packed, "span", span)
    left, right = up(packed), down(packed)
    krylov, sums = pl.pallas_call(
        krylov_kernel,
        out_shape=(kept(STEPS, fields, nx, ny, nz), kept(inner, 1, nz)),
        in_specs=[SMEM] + [VMEM] * 8,
        out_specs=(VMEM, VMEM),
        scratch_shapes=[
            pltpu.VMEM((2, everything, 4 * STEPS, ny, nz), jnp.float32),
            pltpu.VMEM((2, everything, 2, ny, nz), jnp.float32),
            pltpu.VMEM((fields, ny, nz), jnp.float32),
        ],
        compiler_params=pltpu.CompilerParams(vmem_limit_bytes=16 * 2**20),
        name="krylov",
    )(mixing_matrix, *near(before, low, high, after, packed, left, right, basis))
    sums = lax.all_to_all(sums, "inner", 0, 0, tiled=True)
    sums = jnp.broadcast_to(jnp.sum(sums, axis=0, keepdims=True), (outer * span, 1, nz))
    sums = lax.all_to_all(sums, ("outer", "span"), 0, 0, tiled=True)
    return pl.pallas_call(
        functools.partial(finish_kernel, total),
        out_shape=(
            shape_of(count, STEPS),
            shape_of(STEPS, STEPS),
            shape_of(STEPS, fields, nx, ny, nz),
        ),
        in_specs=[VMEM] * 3,
        out_specs=(VMEM, VMEM, VMEM),
        compiler_params=pltpu.CompilerParams(vmem_limit_bytes=16 * 2**20),
        name="finish",
    )(*near(sums, krylov, basis))


def solution(mesh):
    stream, span = mesh.shape["stream"], mesh.shape["span"]
    inner = 1
    while inner * inner < stream * span and stream % (2 * inner) == 0:
        inner *= 2
    outer = stream // inner
    split = Mesh(np.asarray(mesh.devices).reshape(outer, inner, span), ("outer", "inner", "span"))
    field = P(("outer", "inner"), None, "span")
    vectors = P(None, None, ("outer", "inner"), None, "span")
    return jax.shard_map(
        functools.partial(on_device, (outer, inner, span)),
        mesh=split,
        in_specs=(vectors, P(), P(), field, field, field),
        out_specs=(P(), P(), vectors),
        check_vma=False,
    )
```

```python
import functools

import jax
import jax.numpy as jnp
import numpy as np
from jax import lax
from jax.experimental import pallas as pl
from jax.experimental.pallas import tpu as pltpu
from jax.sharding import Mesh
from jax.sharding import PartitionSpec as P

STEPS = 4
LANES = 128
EXTRA = 3
VMEM = pl.BlockSpec(memory_space=pltpu.VMEM)
SMEM = pl.BlockSpec(memory_space=pltpu.SMEM)
HBM = pl.BlockSpec(memory_space=pltpu.HBM)
PAIRS = [(a, b) for a in range(STEPS) for b in range(a, STEPS)]


def lane_index():
    return lax.broadcasted_iota(jnp.int32, (8, LANES), 1)


def row_index():
    return lax.broadcasted_iota(jnp.int32, (8, LANES), 0)


def start_kernel(coeffs, basis, base_speed, span_speed, gain, low, high, held, weights, weight_sem, basis_sems, field_sems):
    count, fields = basis.shape[0], basis.shape[1]
    weight_copy = pltpu.make_async_copy(coeffs, weights, weight_sem)
    weight_copy.start()

    def basis_copy(f):
        return pltpu.make_async_copy(basis.at[:, f], held.at[:, f], basis_sems.at[f])

    for f in range(fields):
        basis_copy(f).start()
    copies = []
    for e, ref in enumerate((base_speed, span_speed, gain)):
        for part, out in enumerate((low, high)):
            copies.append(
                pltpu.make_async_copy(
                    ref.at[pl.ds(part * STEPS, STEPS)], out.at[fields + e], field_sems.at[e, part]
                )
            )
            copies[-1].start()
    weight_copy.wait()
    scale = [weights[m] for m in range(count)]

    def field(f, carry):
        basis_copy(f).wait()
        for x in range(2 * STEPS):
            value = scale[0] * held[0, f, x]
            for m in range(1, count):
                value = value + scale[m] * held[m, f, x]
            (low if x < STEPS else high)[f, x % STEPS] = value
        return carry

    lax.fori_loop(0, fields, field, 0)
    for copy in copies:
        copy.wait()


def pack(tiles, value):
    group = lane_index() // 8
    for r, tile in tiles:
        turned = pltpu.roll(tile, (8 * r + 4) % LANES, 1)
        value = jnp.where(group == r, turned, value)
    return value


def prepare_kernel(mixing, low, high, held, own, old_sums, splat):
    fields = held.shape[1]
    for f in range(fields):
        for g in range(fields):
            splat[f * fields + g] = jnp.full((8, LANES), mixing[f, g], jnp.float32)
    blank = jnp.zeros((8, LANES), jnp.float32)

    def field(f, carry):
        rows = [(STEPS + r, low[f, r]) for r in range(STEPS)]
        rows += [(2 * STEPS + r, high[f, r]) for r in range(STEPS)]
        own[f] = pack(rows, blank)
        return carry

    lax.fori_loop(0, own.shape[0], field, 0)

    def products(f, totals):
        totals = list(totals)
        for x in range(2 * STEPS):
            old = [held[m, f, x] for m in range(STEPS)]
            for i, (a, b) in enumerate(PAIRS):
                totals[i] = totals[i] + old[a] * old[b]
        return tuple(totals)

    totals = lax.fori_loop(0, fields, products, (blank,) * len(PAIRS))
    for i, total in enumerate(totals):
        old_sums[i] = total


def edges_kernel(before, after, own, packed):
    def field(f, carry):
        rows = [(r, before[f, r]) for r in range(STEPS)]
        rows += [(3 * STEPS + r, after[f, r]) for r in range(STEPS)]
        packed[f] = pack(rows, own[f])
        return carry

    lax.fori_loop(0, own.shape[0], field, 0)


def speeds(base, span):
    half_x, half_z = 0.5 * base, 0.5 * span
    return 0.05 - half_x, 0.05 + half_x, 0.05 - half_z, 0.05 + half_z


def walls():
    sub = row_index()
    return (
        jnp.where(sub < 7, 0.05, 0.0).astype(jnp.float32),
        jnp.where(sub > 0, 0.05, 0.0).astype(jnp.float32),
    )


def stencil(splat, items, wall, store):
    fields = len(items[0][0])
    scales = [speeds(item[5], item[6]) for item in items]
    for f in range(fields):
        mixed = [None] * len(items)
        for g in range(fields):
            weight = splat[f * fields + g]
            for i, item in enumerate(items):
                part = weight * item[0][g]
                mixed[i] = part if g == 0 else mixed[i] + part
        for i, (values, x_up, x_down, z_up, z_down, _, _, gain) in enumerate(items):
            c_xu, c_xd, c_zu, c_zd = scales[i]
            v = values[f]
            near_x = c_xu * x_up(f) + c_xd * x_down(f)
            near_z = c_zu * z_up(f) + c_zd * z_down(f)
            near_y = wall[0] * pltpu.roll(v, 7, 0) + wall[1] * pltpu.roll(v, 1, 0)
            store(i, f, (near_x + near_z) + (near_y - 0.3 * v) + gain * mixed[i])


def first_kernel(splat, before, low, high, after, made, coefs):
    fields, rows = before.shape[0] - EXTRA, 4 * STEPS
    parts = (before, low, high, after)
    lane, wall = lane_index(), walls()
    for e in range(EXTRA):
        for r in range(rows):
            coefs[e, r] = parts[r // STEPS][fields + e, r % STEPS]

    def tile(f, r):
        return parts[r // STEPS][f, r % STEPS]

    def item(r):
        values = [tile(f, r) for f in range(fields)]
        return (
            values,
            lambda f: tile(f, r + 1),
            lambda f: tile(f, r - 1),
            lambda f: jnp.where(lane == LANES - 1, 0.0, pltpu.roll(values[f], LANES - 1, 1)),
            lambda f: jnp.where(lane == 0, 0.0, pltpu.roll(values[f], 1, 1)),
            tile(fields, r),
            tile(fields + 1, r),
            tile(fields + 2, r),
        )

    for r in range(1, rows - 1, 2):

        def store(i, f, value, r=r):
            made[f, r + i] = value

        stencil(splat, [item(r), item(r + 1)], wall, store)


def krylov_kernel(
    splat, own, left, right, made, coefs, held, old_sums, krylov, sums, state, rim, inject
):
    fields, rows = held.shape[1], 4 * STEPS
    lane, wall = lane_index(), walls()
    inner = lane % 8 < 4

    def load(f, carry):
        mine = own[f]
        rim[0, f, 0] = jnp.where(inner, left[f], mine)
        rim[0, f, 1] = jnp.where(inner, mine, right[f])
        return carry

    lax.fori_loop(0, fields + EXTRA, load, 0)

    for k in range(STEPS):
        src = state.at[k % 2]
        dst = state.at[(k + 1) % 2]
        rim_src, rim_dst = rim.at[k % 2], rim.at[(k + 1) % 2]
        for f in range(fields):
            inject[f] = jnp.where(lane % 8 == 5, pltpu.roll(rim_src[f, 0], 2, 1), rim_src[f, 1])
        if k + 1 < STEPS:

            def edge(e):
                values = [rim_src[f, e] for f in range(fields)]
                return (
                    values,
                    lambda f: pltpu.roll(values[f], LANES - 8, 1),
                    lambda f: pltpu.roll(values[f], 8, 1),
                    lambda f: pltpu.roll(values[f], LANES - 1, 1),
                    lambda f: pltpu.roll(values[f], 1, 1),
                    rim[0, fields, e],
                    rim[0, fields + 1, e],
                    rim[0, fields + 2, e],
                )

            def edge_store(i, f, value):
                rim_dst[f, i] = value

            stencil(splat, [edge(0), edge(1)], wall, edge_store)

        def turned(f, r):
            return pltpu.roll(inject[f], 123 - 8 * r, 1)

        if k == 0:

            def fix(r, carry):
                _, _, c_zu, c_zd = speeds(coefs[0, r], coefs[1, r])
                scale = jnp.where(lane == LANES - 1, c_zu, jnp.where(lane == 0, c_zd, 0.0))
                for f in range(fields):
                    dst[f, r] = made[f, r] + scale * turned(f, r)
                return carry

            lax.fori_loop(1, rows - 1, fix, 0)
            krylov[0] = dst[:, STEPS : 3 * STEPS]
            continue

        def item(r):
            values = [src[f, r] for f in range(fields)]
            return (
                values,
                lambda f: src[f, r + 1],
                lambda f: src[f, r - 1],
                lambda f: jnp.where(
                    lane == LANES - 1, turned(f, r), pltpu.roll(values[f], LANES - 1, 1)
                ),
                lambda f: jnp.where(lane == 0, turned(f, r), pltpu.roll(values[f], 1, 1)),
                coefs[0, r],
                coefs[1, r],
                coefs[2, r],
            )

        def row(q, carry):
            r = k + 1 + 2 * q

            def store(i, f, value):
                dst[f, r + i] = value

            stencil(splat, [item(r), item(r + 1)], wall, store)
            return carry

        lax.fori_loop(0, (rows - 2 * k - 2) // 2, row, 0)
        krylov[k] = dst[:, STEPS : 3 * STEPS]

    def products(f, totals):
        totals = list(totals)
        for x in range(2 * STEPS):
            new = [krylov[k, f, x] for k in range(STEPS)]
            old = [held[m, f, x] for m in range(STEPS)]
            i = 0
            for a in range(STEPS):
                for b in range(STEPS):
                    totals[i] = totals[i] + old[a] * new[b]
                    i += 1
            for a, b in PAIRS:
                totals[i] = totals[i] + new[a] * new[b]
                i += 1
        return tuple(totals)

    zero = jnp.zeros((8, LANES), jnp.float32)
    totals = lax.fori_loop(0, fields, products, (zero,) * (STEPS * STEPS + len(PAIRS)))
    totals = list(totals) + [old_sums[i] for i in range(len(PAIRS))]
    lines = [jnp.sum(t, axis=0, keepdims=True) for t in totals]
    lines.append(jnp.zeros((LANES - len(lines), LANES), jnp.float32))
    table = jnp.concatenate(lines, axis=0)
    row_sums = lax.dot_general(
        jnp.ones((8, LANES), jnp.float32),
        table,
        (((1,), (1,)), ((), ())),
        precision=lax.Precision.HIGHEST,
        preferred_element_type=jnp.float32,
    )
    for i in range(sums.shape[0]):
        sums[i] = row_sums[0:1]


def finish_kernel(total, parts, krylov, basis, proj_out, factor_out, new_out, buffer, sems):
    fields = basis.shape[1]
    line = parts[0]
    for i in range(1, parts.shape[0]):
        line = line + parts[i]
    line = jnp.broadcast_to(line / total, (8, LANES))
    spread = [
        jnp.broadcast_to(line[:, i : i + 1], (8, LANES))
        for i in range(STEPS * STEPS + 2 * len(PAIRS))
    ]
    proj = [[spread[a * STEPS + b] for b in range(STEPS)] for a in range(STEPS)]
    new_new, old_old = {}, {}
    for i, (a, b) in enumerate(PAIRS):
        new_new[a, b] = spread[STEPS * STEPS + i]
        old_old[a, b] = old_old[b, a] = spread[STEPS * STEPS + len(PAIRS) + i]
    turned = [
        [
            sum(old_old[j, i] * proj[i][k] for i in range(STEPS)) - 2.0 * proj[j][k]
            for k in range(STEPS)
        ]
        for j in range(STEPS)
    ]
    gram = {
        (a, b): new_new[a, b] + sum(proj[j][a] * turned[j][b] for j in range(STEPS))
        for a, b in PAIRS
    }
    lower, inverse = {}, []
    for b in range(STEPS):
        for a in range(b, STEPS):
            value = gram[b, a]
            for c in range(b):
                value = value - lower[a, c] * lower[b, c]
            if a == b:
                lower[a, b] = jnp.sqrt(value)
                inverse.append(1.0 / lower[a, b])
            else:
                lower[a, b] = value * inverse[b]
    lane, sub = lane_index(), row_index()
    proj_tile = jnp.zeros((8, LANES), jnp.float32)
    factor_tile = proj_tile
    for a in range(STEPS):
        for b in range(STEPS):
            here = (sub == a) & (lane == b)
            proj_tile = jnp.where(here, proj[a][b], proj_tile)
            if b >= a:
                factor_tile = jnp.where(here, lower[b, a], factor_tile)
    proj_out[...] = proj_tile[:STEPS, :STEPS]
    factor_out[...] = factor_tile[:STEPS, :STEPS]

    def field(f, carry):
        for x in range(2 * STEPS):
            old = [basis[m, f, x] for m in range(STEPS)]
            made = []
            for k in range(STEPS):
                value = krylov[k, f, x]
                for m in range(STEPS):
                    value = value - proj[m][k] * old[m]
                for c in range(k):
                    value = value - lower[k, c] * made[c]
                made.append(value * inverse[k])
                buffer[k, f, x] = made[k]
        out_copy(f).start()
        return carry

    def out_copy(f):
        return pltpu.make_async_copy(buffer.at[:, f], new_out.at[:, f], sems.at[f])

    lax.fori_loop(0, fields, field, 0)
    for f in range(fields):
        out_copy(f).wait()


def far(*arrays):
    return [pltpu.with_memory_space_constraint(a, pltpu.HBM) for a in arrays]


def ring(axes, size):
    up = [(i, (i + 1) % size) for i in range(size)]
    down = [(j, i) for i, j in up]
    return lambda v: lax.ppermute(v, axes, up), lambda v: lax.ppermute(v, axes, down)


def shape_of(*dims):
    return jax.ShapeDtypeStruct(dims, jnp.float32)


def kept(*dims):
    return pltpu.VMEM(dims, jnp.float32)


def near(*arrays):
    return [pltpu.with_memory_space_constraint(a, pltpu.VMEM) for a in arrays]


def on_device(sizes, basis, coeffs, mixing_matrix, base_speed, span_speed, polymer_gain):
    outer, inner, span = sizes
    count, fields, nx, ny, nz = basis.shape
    total = float(basis[0].size * outer * inner * span)
    everything = fields + EXTRA
    slab = kept(everything, STEPS, ny, nz)
    vectors = (count, fields, nx, ny, nz)
    params = pltpu.CompilerParams(vmem_limit_bytes=16 * 2**20)
    low, high, held = pl.pallas_call(
        start_kernel,
        out_shape=(slab, slab, kept(*vectors)),
        in_specs=[HBM] * 5,
        out_specs=(VMEM,) * 3,
        scratch_shapes=[
            pltpu.SMEM((count,), jnp.float32),
            pltpu.SemaphoreType.DMA(()),
            pltpu.SemaphoreType.DMA((fields,)),
            pltpu.SemaphoreType.DMA((EXTRA, 2)),
        ],
        compiler_params=params,
        name="start",
    )(*far(coeffs, basis, base_speed, span_speed, polymer_gain))
    up, down = ring(("outer", "inner"), outer * inner)
    before, after = up(high), down(low)
    own, old_sums, splat = pl.pallas_call(
        prepare_kernel,
        out_shape=(
            kept(everything, ny, nz),
            kept(len(PAIRS), ny, nz),
            kept(fields * fields, ny, nz),
        ),
        in_specs=[SMEM] + [VMEM] * 3,
        out_specs=(VMEM,) * 3,
        compiler_params=params,
        name="prepare",
    )(mixing_matrix, *near(low, high, held))
    packed = pl.pallas_call(
        edges_kernel,
        out_shape=kept(everything, ny, nz),
        in_specs=[VMEM] * 3,
        out_specs=VMEM,
        compiler_params=params,
        name="edges",
    )(*near(before, after, own))
    up, down = ring("span", span)
    left, right = up(packed), down(packed)
    made, coefs = pl.pallas_call(
        first_kernel,
        out_shape=(kept(fields, 4 * STEPS, ny, nz), kept(EXTRA, 4 * STEPS, ny, nz)),
        in_specs=[VMEM] * 5,
        out_specs=(VMEM,) * 2,
        compiler_params=params,
        name="first",
    )(*near(splat, before, low, high, after))
    krylov, sums = pl.pallas_call(
        krylov_kernel,
        out_shape=(kept(*vectors), kept(inner, 1, nz)),
        in_specs=[VMEM] * 8,
        out_specs=(VMEM,) * 2,
        scratch_shapes=[
            pltpu.VMEM((2, fields, 4 * STEPS, ny, nz), jnp.float32),
            pltpu.VMEM((2, everything, 2, ny, nz), jnp.float32),
            pltpu.VMEM((fields, ny, nz), jnp.float32),
        ],
        compiler_params=params,
        name="krylov",
    )(*near(splat, packed, left, right, made, coefs, held, old_sums))
    sums = lax.all_to_all(sums, "inner", 0, 0, tiled=True)
    sums = jnp.broadcast_to(jnp.sum(sums, axis=0, keepdims=True), (outer * span, 1, nz))
    sums = lax.all_to_all(sums, ("outer", "span"), 0, 0, tiled=True)
    return pl.pallas_call(
        functools.partial(finish_kernel, total),
        out_shape=(shape_of(count, STEPS), shape_of(STEPS, STEPS), shape_of(*vectors)),
        in_specs=[VMEM] * 3,
        out_specs=(VMEM, VMEM, HBM),
        scratch_shapes=[
            pltpu.VMEM(vectors, jnp.float32),
            pltpu.SemaphoreType.DMA((fields,)),
        ],
        compiler_params=params,
        name="finish",
    )(*near(sums, krylov, held))


def solution(mesh):
    stream, span = mesh.shape["stream"], mesh.shape["span"]
    inner = 1
    while inner * inner < stream * span and stream % (2 * inner) == 0:
        inner *= 2
    outer = stream // inner
    split = Mesh(np.asarray(mesh.devices).reshape(outer, inner, span), ("outer", "inner", "span"))
    field = P(("outer", "inner"), None, "span")
    vectors = P(None, None, ("outer", "inner"), None, "span")
    return jax.shard_map(
        functools.partial(on_device, (outer, inner, span)),
        mesh=split,
        in_specs=(vectors, P(), P(), field, field, field),
        out_specs=(P(), P(), vectors),
        check_vma=False,
    )
```

```python
import functools

import jax
import jax.numpy as jnp
import numpy as np
from jax import lax
from jax.experimental import pallas as pl
from jax.experimental.pallas import tpu as pltpu
from jax.sharding import Mesh
from jax.sharding import PartitionSpec as P

STEPS = 4
LANES = 128
EXTRA = 3
VMEM = pl.BlockSpec(memory_space=pltpu.VMEM)
SMEM = pl.BlockSpec(memory_space=pltpu.SMEM)
HBM = pl.BlockSpec(memory_space=pltpu.HBM)
PAIRS = [(a, b) for a in range(STEPS) for b in range(a, STEPS)]


def lane_index():
    return lax.broadcasted_iota(jnp.int32, (8, LANES), 1)


def row_index():
    return lax.broadcasted_iota(jnp.int32, (8, LANES), 0)


def parity():
    return lax.axis_index("inner") % 2


def start_kernel(
    coeffs, basis, base_speed, span_speed, gain, cross, chip, held, weights, weight_sem, basis_sems, field_sems
):
    count, fields = basis.shape[0], basis.shape[1]
    half = fields // 2
    first_row = STEPS * parity()
    sides = ((cross, first_row), (chip, STEPS - first_row))
    weight_copy = pltpu.make_async_copy(coeffs, weights, weight_sem)
    weight_copy.start()
    waves = []
    for w in range(2):
        span = pl.ds(w * half, half)
        waves.append(
            [
                pltpu.make_async_copy(basis.at[m, span], held.at[m, span], basis_sems.at[w, m])
                for m in range(count)
            ]
        )
        for copy in waves[w]:
            copy.start()
    copies = []
    for e, ref in enumerate((base_speed, span_speed, gain)):
        for i, (out, row) in enumerate(sides):
            copies.append(
                pltpu.make_async_copy(
                    ref.at[pl.ds(row, STEPS)], out.at[fields + e], field_sems.at[e, i]
                )
            )
            copies[-1].start()
    weight_copy.wait()
    scale = [weights[m] for m in range(count)]

    def field(f, carry):
        for r in range(STEPS):
            for out, row in sides:
                value = scale[0] * held[0, f, row + r]
                for m in range(1, count):
                    value = value + scale[m] * held[m, f, row + r]
                out[f, r] = value
        return carry

    for w in range(2):
        for copy in waves[w]:
            copy.wait()
        lax.fori_loop(w * half, (w + 1) * half, field, 0)
    for copy in copies:
        copy.wait()


def pack(tiles, value):
    group = lane_index() // 8
    for r, tile in tiles:
        value = jnp.where(group == r, pltpu.roll(tile, 8 * r + 4, 1), value)
    return value


def prepare_kernel(mixing, cross, chip, held, own, old_sums, splat):
    fields = held.shape[1]
    for f in range(fields):
        for g in range(fields):
            splat[f * fields + g] = jnp.full((8, LANES), mixing[f, g], jnp.float32)
    blank = jnp.zeros((8, LANES), jnp.float32)
    side = STEPS * parity()

    def field(f, carry):
        rows = [(STEPS + side + r, cross[f, r]) for r in range(STEPS)]
        rows += [(2 * STEPS - side + r, chip[f, r]) for r in range(STEPS)]
        own[f] = pack(rows, blank)
        return carry

    lax.fori_loop(0, own.shape[0], field, 0)

    def products(f, totals):
        totals = list(totals)
        for x in range(2 * STEPS):
            old = [held[m, f, x] for m in range(STEPS)]
            for i, (a, b) in enumerate(PAIRS):
                totals[i] = totals[i] + old[a] * old[b]
        return tuple(totals)

    totals = lax.fori_loop(0, fields, products, (blank,) * len(PAIRS))
    for i, total in enumerate(totals):
        old_sums[i] = total


def edges_kernel(from_cross, from_chip, own, packed):
    side = 3 * STEPS * parity()
    for f in range(own.shape[0]):
        rows = [(side + r, from_cross[f, r]) for r in range(STEPS)]
        rows += [(3 * STEPS - side + r, from_chip[f, r]) for r in range(STEPS)]
        packed[f] = pack(rows, own[f])


def speeds(base, span):
    half_x, half_z = 0.5 * base, 0.5 * span
    return 0.05 - half_x, 0.05 + half_x, 0.05 - half_z, 0.05 + half_z


def walls():
    sub = row_index()
    return (
        jnp.where(sub < 7, 0.05, 0.0).astype(jnp.float32),
        jnp.where(sub > 0, 0.05, 0.0).astype(jnp.float32),
    )


def stencil(splat, items, wall, store):
    fields = len(items[0][0])
    scales = [speeds(item[5], item[6]) for item in items]
    for f in range(fields):
        mixed = [None] * len(items)
        for g in range(fields):
            weight = splat[f * fields + g]
            for i, item in enumerate(items):
                part = weight * item[0][g]
                mixed[i] = part if g == 0 else mixed[i] + part
        for i, (values, x_up, x_down, z_up, z_down, _, _, gain) in enumerate(items):
            c_xu, c_xd, c_zu, c_zd = scales[i]
            v = values[f]
            near_x = c_xu * x_up(f) + c_xd * x_down(f)
            near_z = c_zu * z_up(f) + c_zd * z_down(f)
            near_y = wall[0] * pltpu.roll(v, 7, 0) + wall[1] * pltpu.roll(v, 1, 0)
            store(i, f, (near_x + near_z) + (near_y - 0.3 * v) + gain * mixed[i])


def first_kernel(splat, from_cross, cross, chip, from_chip, made, coefs, slabs):
    fields, rows = cross.shape[0] - EXTRA, 4 * STEPS
    lane, wall = lane_index(), walls()
    side = STEPS * parity()
    for ref, row in (
        (from_cross, 3 * side),
        (cross, STEPS + side),
        (chip, 2 * STEPS - side),
        (from_chip, 3 * (STEPS - side)),
    ):
        slabs[:, pl.ds(row, STEPS)] = ref[...]
    coefs[...] = slabs[fields:]

    def item(r):
        values = [slabs[f, r] for f in range(fields)]
        return (
            values,
            lambda f: slabs[f, r + 1],
            lambda f: slabs[f, r - 1],
            lambda f: jnp.where(lane == LANES - 1, 0.0, pltpu.roll(values[f], LANES - 1, 1)),
            lambda f: jnp.where(lane == 0, 0.0, pltpu.roll(values[f], 1, 1)),
            slabs[fields, r],
            slabs[fields + 1, r],
            slabs[fields + 2, r],
        )

    for r in range(1, rows - 1, 2):

        def store(i, f, value, r=r):
            made[f, r + i] = value

        stencil(splat, [item(r), item(r + 1)], wall, store)


def krylov_kernel(
    splat, own, left, right, made, coefs, held, old_sums, krylov, sums, outer_rows, rim, inject
):
    fields, rows = held.shape[1], 4 * STEPS
    lane, wall = lane_index(), walls()
    inner = lane % 8 < 4

    def place(k, r):
        if STEPS <= r < 3 * STEPS:
            return krylov.at[k], r - STEPS
        return outer_rows.at[k % 2], r if r < STEPS else r - 2 * STEPS

    for f in range(fields + EXTRA):
        mine = own[f]
        rim[0, f, 0] = jnp.where(inner, left[f], mine)
        rim[0, f, 1] = jnp.where(inner, mine, right[f])

    for k in range(STEPS):
        rim_src, rim_dst = rim.at[k % 2], rim.at[(k + 1) % 2]
        for f in range(fields):
            inject[f] = jnp.where(lane % 8 == 5, pltpu.roll(rim_src[f, 0], 2, 1), rim_src[f, 1])
        if k + 1 < STEPS:

            def edge(e):
                values = [rim_src[f, e] for f in range(fields)]
                return (
                    values,
                    lambda f: pltpu.roll(values[f], LANES - 8, 1),
                    lambda f: pltpu.roll(values[f], 8, 1),
                    lambda f: pltpu.roll(values[f], LANES - 1, 1),
                    lambda f: pltpu.roll(values[f], 1, 1),
                    rim[0, fields, e],
                    rim[0, fields + 1, e],
                    rim[0, fields + 2, e],
                )

            def edge_store(i, f, value):
                rim_dst[f, i] = value

            stencil(splat, [edge(0), edge(1)], wall, edge_store)

        def turned(f, r):
            return pltpu.roll(inject[f], 123 - 8 * r, 1)

        if k == 0:
            for r in range(1, rows - 1):
                _, _, c_zu, c_zd = speeds(coefs[0, r], coefs[1, r])
                scale = jnp.where(lane == LANES - 1, c_zu, jnp.where(lane == 0, c_zd, 0.0))
                ref, at = place(0, r)
                for f in range(fields):
                    ref[f, at] = made[f, r] + scale * turned(f, r)
            continue

        def tile(f, r):
            ref, at = place(k - 1, r)
            return ref[f, at]

        def item(r):
            values = [tile(f, r) for f in range(fields)]
            return (
                values,
                lambda f: tile(f, r + 1),
                lambda f: tile(f, r - 1),
                lambda f: jnp.where(
                    lane == LANES - 1, turned(f, r), pltpu.roll(values[f], LANES - 1, 1)
                ),
                lambda f: jnp.where(lane == 0, turned(f, r), pltpu.roll(values[f], 1, 1)),
                coefs[0, r],
                coefs[1, r],
                coefs[2, r],
            )

        for r in range(k + 1, rows - k - 1, 2):

            def store(i, f, value):
                ref, at = place(k, r + i)
                ref[f, at] = value

            stencil(splat, [item(r), item(r + 1)], wall, store)

    def products(f, totals):
        totals = list(totals)
        for x in range(2 * STEPS):
            new = [krylov[k, f, x] for k in range(STEPS)]
            old = [held[m, f, x] for m in range(STEPS)]
            i = 0
            for a in range(STEPS):
                for b in range(STEPS):
                    totals[i] = totals[i] + old[a] * new[b]
                    i += 1
            for a, b in PAIRS:
                totals[i] = totals[i] + new[a] * new[b]
                i += 1
        return tuple(totals)

    zero = jnp.zeros((8, LANES), jnp.float32)
    totals = lax.fori_loop(0, fields, products, (zero,) * (STEPS * STEPS + len(PAIRS)))
    totals = list(totals) + [old_sums[i] for i in range(len(PAIRS))]
    lines = [jnp.sum(t, axis=0, keepdims=True) for t in totals]
    lines.append(jnp.zeros((LANES - len(lines), LANES), jnp.float32))
    table = jnp.concatenate(lines, axis=0)
    row_sums = lax.dot_general(
        jnp.ones((8, LANES), jnp.float32),
        table,
        (((1,), (1,)), ((), ())),
        precision=lax.Precision.HIGHEST,
        preferred_element_type=jnp.float32,
    )
    for i in range(sums.shape[0]):
        sums[i] = row_sums[0:1]


def finish_kernel(total, parts, krylov, basis, proj_out, factor_out, new_out, buffer, sems):
    fields = basis.shape[1]
    line = parts[0]
    for i in range(1, parts.shape[0]):
        line = line + parts[i]
    line = jnp.broadcast_to(line / total, (8, LANES))
    spread = [
        jnp.broadcast_to(line[:, i : i + 1], (8, LANES))
        for i in range(STEPS * STEPS + 2 * len(PAIRS))
    ]
    proj = [[spread[a * STEPS + b] for b in range(STEPS)] for a in range(STEPS)]
    new_new, old_old = {}, {}
    for i, (a, b) in enumerate(PAIRS):
        new_new[a, b] = spread[STEPS * STEPS + i]
        old_old[a, b] = old_old[b, a] = spread[STEPS * STEPS + len(PAIRS) + i]
    turned = [
        [
            sum(old_old[j, i] * proj[i][k] for i in range(STEPS)) - 2.0 * proj[j][k]
            for k in range(STEPS)
        ]
        for j in range(STEPS)
    ]
    gram = {
        (a, b): new_new[a, b] + sum(proj[j][a] * turned[j][b] for j in range(STEPS))
        for a, b in PAIRS
    }
    lower, inverse = {}, []
    for b in range(STEPS):
        for a in range(b, STEPS):
            value = gram[b, a]
            for c in range(b):
                value = value - lower[a, c] * lower[b, c]
            if a == b:
                lower[a, b] = jnp.sqrt(value)
                inverse.append(1.0 / lower[a, b])
            else:
                lower[a, b] = value * inverse[b]
    lane, sub = lane_index(), row_index()
    proj_tile = jnp.zeros((8, LANES), jnp.float32)
    factor_tile = proj_tile
    for a in range(STEPS):
        for b in range(STEPS):
            here = (sub == a) & (lane == b)
            proj_tile = jnp.where(here, proj[a][b], proj_tile)
            if b >= a:
                factor_tile = jnp.where(here, lower[b, a], factor_tile)
    proj_out[...] = proj_tile[:STEPS, :STEPS]
    factor_out[...] = factor_tile[:STEPS, :STEPS]

    def field(f, carry):
        for x in range(2 * STEPS):
            old = [basis[m, f, x] for m in range(STEPS)]
            made = []
            for k in range(STEPS):
                value = krylov[k, f, x]
                for m in range(STEPS):
                    value = value - proj[m][k] * old[m]
                for c in range(k):
                    value = value - lower[k, c] * made[c]
                made.append(value * inverse[k])
                buffer[k, f, x] = made[k]
        return carry

    half = fields // 2
    copies = []
    for w in range(2):
        lax.fori_loop(w * half, (w + 1) * half, field, 0)
        span = pl.ds(w * half, half)
        for k in range(STEPS):
            copies.append(
                pltpu.make_async_copy(buffer.at[k, span], new_out.at[k, span], sems.at[w, k])
            )
            copies[-1].start()
    for copy in copies:
        copy.wait()


def far(*arrays):
    return [pltpu.with_memory_space_constraint(a, pltpu.HBM) for a in arrays]


def swaps(size, first):
    pairs = [(i, (i + 1) % size) for i in range(first, size, 2)]
    return pairs + [(j, i) for i, j in pairs]


def ring(axes, size):
    up = [(i, (i + 1) % size) for i in range(size)]
    down = [(j, i) for i, j in up]
    return lambda v: lax.ppermute(v, axes, up), lambda v: lax.ppermute(v, axes, down)


def shape_of(*dims):
    return jax.ShapeDtypeStruct(dims, jnp.float32)


def kept(*dims):
    return pltpu.VMEM(dims, jnp.float32)


def near(*arrays):
    return [pltpu.with_memory_space_constraint(a, pltpu.VMEM) for a in arrays]


def on_device(sizes, basis, coeffs, mixing_matrix, base_speed, span_speed, polymer_gain):
    outer, inner, span = sizes
    count, fields, nx, ny, nz = basis.shape
    total = float(basis[0].size * outer * inner * span)
    everything = fields + EXTRA
    slab = kept(everything, STEPS, ny, nz)
    vectors = (count, fields, nx, ny, nz)
    params = pltpu.CompilerParams(vmem_limit_bytes=16 * 2**20)
    cross, chip, held = pl.pallas_call(
        start_kernel,
        out_shape=(slab, slab, kept(*vectors)),
        in_specs=[HBM] * 5,
        out_specs=(VMEM,) * 3,
        scratch_shapes=[
            pltpu.SMEM((count,), jnp.float32),
            pltpu.SemaphoreType.DMA(()),
            pltpu.SemaphoreType.DMA((2, count)),
            pltpu.SemaphoreType.DMA((EXTRA, 2)),
        ],
        compiler_params=params,
        name="start",
    )(*far(coeffs, basis, base_speed, span_speed, polymer_gain))
    stream = ("outer", "inner")
    from_cross = lax.ppermute(cross, stream, swaps(outer * inner, 1))
    from_chip = lax.ppermute(chip, stream, swaps(outer * inner, 0))
    own, old_sums, splat = pl.pallas_call(
        prepare_kernel,
        out_shape=(
            kept(everything, ny, nz),
            kept(len(PAIRS), ny, nz),
            kept(fields * fields, ny, nz),
        ),
        in_specs=[SMEM] + [VMEM] * 3,
        out_specs=(VMEM,) * 3,
        compiler_params=params,
        name="prepare",
    )(mixing_matrix, *near(cross, chip, held))
    packed = pl.pallas_call(
        edges_kernel,
        out_shape=kept(everything, ny, nz),
        in_specs=[VMEM] * 3,
        out_specs=VMEM,
        compiler_params=params,
        name="edges",
    )(*near(from_cross, from_chip, own))
    up, down = ring("span", span)
    left, right = up(packed), down(packed)
    made, coefs = pl.pallas_call(
        first_kernel,
        out_shape=(kept(fields, 4 * STEPS, ny, nz), kept(EXTRA, 4 * STEPS, ny, nz)),
        in_specs=[VMEM] * 5,
        out_specs=(VMEM,) * 2,
        scratch_shapes=[pltpu.VMEM((everything, 4 * STEPS, ny, nz), jnp.float32)],
        compiler_params=params,
        name="first",
    )(*near(splat, from_cross, cross, chip, from_chip))
    krylov, sums = pl.pallas_call(
        krylov_kernel,
        out_shape=(kept(*vectors), kept(inner, 1, nz)),
        in_specs=[VMEM] * 8,
        out_specs=(VMEM,) * 2,
        scratch_shapes=[
            pltpu.VMEM((2, fields, 2 * STEPS, ny, nz), jnp.float32),
            pltpu.VMEM((2, everything, 2, ny, nz), jnp.float32),
            pltpu.VMEM((fields, ny, nz), jnp.float32),
        ],
        compiler_params=params,
        name="krylov",
    )(*near(splat, packed, left, right, made, coefs, held, old_sums))
    sums = lax.all_to_all(sums, "inner", 0, 0, tiled=True)
    sums = jnp.broadcast_to(jnp.sum(sums, axis=0, keepdims=True), (outer * span, 1, nz))
    sums = lax.all_to_all(sums, ("outer", "span"), 0, 0, tiled=True)
    return pl.pallas_call(
        functools.partial(finish_kernel, total),
        out_shape=(shape_of(count, STEPS), shape_of(STEPS, STEPS), shape_of(*vectors)),
        in_specs=[VMEM] * 3,
        out_specs=(VMEM, VMEM, HBM),
        scratch_shapes=[
            pltpu.VMEM(vectors, jnp.float32),
            pltpu.SemaphoreType.DMA((2, STEPS)),
        ],
        compiler_params=params,
        name="finish",
    )(*near(sums, krylov, held))


def solution(mesh):
    stream, span = mesh.shape["stream"], mesh.shape["span"]
    inner = 1
    while inner * inner < stream * span and stream % (2 * inner) == 0:
        inner *= 2
    outer = stream // inner
    split = Mesh(np.asarray(mesh.devices).reshape(outer, inner, span), ("outer", "inner", "span"))
    field = P(("outer", "inner"), None, "span")
    vectors = P(None, None, ("outer", "inner"), None, "span")
    return jax.shard_map(
        functools.partial(on_device, (outer, inner, span)),
        mesh=split,
        in_specs=(vectors, P(), P(), field, field, field),
        out_specs=(P(), P(), vectors),
        check_vma=False,
    )
```

```python
import functools

import jax
import jax.numpy as jnp
import numpy as np
from jax import lax
from jax.experimental import pallas as pl
from jax.experimental.pallas import tpu as pltpu
from jax.sharding import Mesh
from jax.sharding import PartitionSpec as P

STEPS = 4
LANES = 128
EXTRA = 3
VMEM = pl.BlockSpec(memory_space=pltpu.VMEM)
SMEM = pl.BlockSpec(memory_space=pltpu.SMEM)
HBM = pl.BlockSpec(memory_space=pltpu.HBM)
PAIRS = [(a, b) for a in range(STEPS) for b in range(a, STEPS)]


def lane_index():
    return lax.broadcasted_iota(jnp.int32, (8, LANES), 1)


def row_index():
    return lax.broadcasted_iota(jnp.int32, (8, LANES), 0)


def parity():
    return lax.axis_index("inner") % 2


def start_kernel(
    coeffs, basis, base_speed, span_speed, gain, cross, chip, held, weights, weight_sem, basis_sems, field_sems
):
    count, fields = basis.shape[0], basis.shape[1]
    half = fields // 2
    first_row = STEPS * parity()
    sides = ((cross, first_row), (chip, STEPS - first_row))
    weight_copy = pltpu.make_async_copy(coeffs, weights, weight_sem)
    weight_copy.start()
    waves = []
    for w in range(2):
        span = pl.ds(w * half, half)
        waves.append(
            [
                pltpu.make_async_copy(basis.at[m, span], held.at[m, span], basis_sems.at[w, m])
                for m in range(count)
            ]
        )
        for copy in waves[w]:
            copy.start()
    copies = []
    for e, ref in enumerate((base_speed, span_speed, gain)):
        for i, (out, row) in enumerate(sides):
            copies.append(
                pltpu.make_async_copy(
                    ref.at[pl.ds(row, STEPS)], out.at[fields + e], field_sems.at[e, i]
                )
            )
            copies[-1].start()
    weight_copy.wait()
    scale = [weights[m] for m in range(count)]

    def field(f, carry):
        for r in range(STEPS):
            for out, row in sides:
                value = scale[0] * held[0, f, row + r]
                for m in range(1, count):
                    value = value + scale[m] * held[m, f, row + r]
                out[f, r] = value
        return carry

    for w in range(2):
        for copy in waves[w]:
            copy.wait()
        lax.fori_loop(w * half, (w + 1) * half, field, 0)
    for copy in copies:
        copy.wait()


def pack(tiles, value):
    group = lane_index() // 8
    for r, tile in tiles:
        value = jnp.where(group == r, pltpu.roll(tile, 8 * r + 4, 1), value)
    return value


def own_edges_kernel(cross, chip, own):
    side = STEPS * parity()
    for f in range(own.shape[0]):
        rows = [(STEPS + side + r, cross[f, r]) for r in range(STEPS)]
        rows += [(2 * STEPS - side + r, chip[f, r]) for r in range(STEPS)]
        own[f] = pack(rows, jnp.zeros((8, LANES), jnp.float32))


def edges_kernel(from_cross, from_chip, own, packed, to_right, to_left):
    side = 3 * STEPS * parity()
    made = []
    for f in range(own.shape[0]):
        rows = [(side + r, from_cross[f, r]) for r in range(STEPS)]
        rows += [(3 * STEPS - side + r, from_chip[f, r]) for r in range(STEPS)]
        made.append(pack(rows, own[f]))
        packed[f] = made[f]
    inner = lane_index() % 8 < 4
    for q in range(to_right.shape[0]):
        even, odd = made[2 * q], made[min(2 * q + 1, len(made) - 1)]
        to_right[q] = jnp.where(inner, even, pltpu.roll(odd, 4, 1))
        to_left[q] = jnp.where(inner, pltpu.roll(odd, LANES - 4, 1), even)


def speeds(base, span):
    half_x, half_z = 0.5 * base, 0.5 * span
    return 0.05 - half_x, 0.05 + half_x, 0.05 - half_z, 0.05 + half_z


def walls():
    sub = row_index()
    return (
        jnp.where(sub < 7, 0.05, 0.0).astype(jnp.float32),
        jnp.where(sub > 0, 0.05, 0.0).astype(jnp.float32),
    )


def stencil(splat, items, wall, store):
    fields = len(items[0][0])
    scales = [speeds(item[5], item[6]) for item in items]
    for f in range(fields):
        mixed = [None] * len(items)
        for g in range(fields):
            weight = splat[f * fields + g]
            for i, item in enumerate(items):
                part = weight * item[0][g]
                mixed[i] = part if g == 0 else mixed[i] + part
        for i, (values, x_up, x_down, z_up, z_down, _, _, gain) in enumerate(items):
            c_xu, c_xd, c_zu, c_zd = scales[i]
            v = values[f]
            near_x = c_xu * x_up(f) + c_xd * x_down(f)
            near_z = c_zu * z_up(f) + c_zd * z_down(f)
            near_y = wall[0] * pltpu.roll(v, 7, 0) + wall[1] * pltpu.roll(v, 1, 0)
            store(i, f, (near_x + near_z) + (near_y - 0.3 * v) + gain * mixed[i])


def first_kernel(
    mixing, from_cross, cross, chip, from_chip, held, made, coefs, splat, old_sums, slabs
):
    fields, rows = cross.shape[0] - EXTRA, 4 * STEPS
    lane, wall = lane_index(), walls()
    side = STEPS * parity()
    for f in range(fields):
        for g in range(fields):
            splat[f * fields + g] = jnp.full((8, LANES), mixing[f, g], jnp.float32)
    for ref, row in (
        (from_cross, 3 * side),
        (cross, STEPS + side),
        (chip, 2 * STEPS - side),
        (from_chip, 3 * (STEPS - side)),
    ):
        slabs[:, pl.ds(row, STEPS)] = ref[...]
    coefs[...] = slabs[fields:]

    def item(r):
        values = [slabs[f, r] for f in range(fields)]
        return (
            values,
            lambda f: slabs[f, r + 1],
            lambda f: slabs[f, r - 1],
            lambda f: jnp.where(lane == LANES - 1, 0.0, pltpu.roll(values[f], LANES - 1, 1)),
            lambda f: jnp.where(lane == 0, 0.0, pltpu.roll(values[f], 1, 1)),
            slabs[fields, r],
            slabs[fields + 1, r],
            slabs[fields + 2, r],
        )

    for r in range(1, rows - 1, 2):

        def store(i, f, value, r=r):
            made[f, r + i] = value

        stencil(splat, [item(r), item(r + 1)], wall, store)

    def products(f, totals):
        totals = list(totals)
        for x in range(2 * STEPS):
            old = [held[m, f, x] for m in range(STEPS)]
            for i, (a, b) in enumerate(PAIRS):
                totals[i] = totals[i] + old[a] * old[b]
        return tuple(totals)

    blank = jnp.zeros((8, LANES), jnp.float32)
    for i, total in enumerate(lax.fori_loop(0, fields, products, (blank,) * len(PAIRS))):
        old_sums[i] = total


def krylov_kernel(
    splat, own, from_left, from_right, made, coefs, held, old_sums, krylov, sums, outer_rows, rim, inject
):
    fields, rows = held.shape[1], 4 * STEPS
    lane, wall = lane_index(), walls()
    inner = lane % 8 < 4

    def place(k, r):
        if STEPS <= r < 3 * STEPS:
            return krylov.at[k], r - STEPS
        return outer_rows.at[k % 2], r if r < STEPS else r - 2 * STEPS

    for f in range(fields + EXTRA):
        mine, left, right = own[f], from_left[f // 2], from_right[f // 2]
        if f % 2:
            left, right = pltpu.roll(left, LANES - 4, 1), pltpu.roll(right, 4, 1)
        rim[0, f, 0] = jnp.where(inner, left, mine)
        rim[0, f, 1] = jnp.where(inner, mine, right)

    for k in range(STEPS):
        rim_src, rim_dst = rim.at[k % 2], rim.at[(k + 1) % 2]
        for f in range(fields):
            inject[f] = jnp.where(lane % 8 == 5, pltpu.roll(rim_src[f, 0], 2, 1), rim_src[f, 1])
        if k + 1 < STEPS:

            def edge(e):
                values = [rim_src[f, e] for f in range(fields)]
                return (
                    values,
                    lambda f: pltpu.roll(values[f], LANES - 8, 1),
                    lambda f: pltpu.roll(values[f], 8, 1),
                    lambda f: pltpu.roll(values[f], LANES - 1, 1),
                    lambda f: pltpu.roll(values[f], 1, 1),
                    rim[0, fields, e],
                    rim[0, fields + 1, e],
                    rim[0, fields + 2, e],
                )

            def edge_store(i, f, value):
                rim_dst[f, i] = value

            stencil(splat, [edge(0), edge(1)], wall, edge_store)

        def turned(f, r):
            return pltpu.roll(inject[f], 123 - 8 * r, 1)

        if k == 0:
            for r in range(1, rows - 1):
                _, _, c_zu, c_zd = speeds(coefs[0, r], coefs[1, r])
                scale = jnp.where(lane == LANES - 1, c_zu, jnp.where(lane == 0, c_zd, 0.0))
                ref, at = place(0, r)
                for f in range(fields):
                    ref[f, at] = made[f, r] + scale * turned(f, r)
            continue

        def tile(f, r):
            ref, at = place(k - 1, r)
            return ref[f, at]

        def item(r):
            values = [tile(f, r) for f in range(fields)]
            return (
                values,
                lambda f: tile(f, r + 1),
                lambda f: tile(f, r - 1),
                lambda f: jnp.where(
                    lane == LANES - 1, turned(f, r), pltpu.roll(values[f], LANES - 1, 1)
                ),
                lambda f: jnp.where(lane == 0, turned(f, r), pltpu.roll(values[f], 1, 1)),
                coefs[0, r],
                coefs[1, r],
                coefs[2, r],
            )

        for r in range(k + 1, rows - k - 1, 2):

            def store(i, f, value):
                ref, at = place(k, r + i)
                ref[f, at] = value

            stencil(splat, [item(r), item(r + 1)], wall, store)

    def products(f, totals):
        totals = list(totals)
        for x in range(2 * STEPS):
            new = [krylov[k, f, x] for k in range(STEPS)]
            old = [held[m, f, x] for m in range(STEPS)]
            i = 0
            for a in range(STEPS):
                for b in range(STEPS):
                    totals[i] = totals[i] + old[a] * new[b]
                    i += 1
            for a, b in PAIRS:
                totals[i] = totals[i] + new[a] * new[b]
                i += 1
        return tuple(totals)

    zero = jnp.zeros((8, LANES), jnp.float32)
    totals = (zero,) * (STEPS * STEPS + len(PAIRS))
    for f in range(fields):
        totals = products(f, totals)
    totals = list(totals) + [old_sums[i] for i in range(len(PAIRS))]
    lines = [jnp.sum(t, axis=0, keepdims=True) for t in totals]
    lines.append(jnp.zeros((LANES - len(lines), LANES), jnp.float32))
    table = jnp.concatenate(lines, axis=0)
    row_sums = lax.dot_general(
        jnp.ones((8, LANES), jnp.float32),
        table,
        (((1,), (1,)), ((), ())),
        precision=lax.Precision.HIGHEST,
        preferred_element_type=jnp.float32,
    )
    for i in range(sums.shape[0]):
        sums[i] = row_sums[0:1]


def finish_kernel(total, parts, krylov, basis, proj_out, factor_out, new_out):
    fields = basis.shape[1]
    line = parts[0]
    for i in range(1, parts.shape[0]):
        line = line + parts[i]
    line = jnp.broadcast_to(line / total, (8, LANES))
    spread = [
        jnp.broadcast_to(line[:, i : i + 1], (8, LANES))
        for i in range(STEPS * STEPS + 2 * len(PAIRS))
    ]
    proj = [[spread[a * STEPS + b] for b in range(STEPS)] for a in range(STEPS)]
    new_new, old_old = {}, {}
    for i, (a, b) in enumerate(PAIRS):
        new_new[a, b] = spread[STEPS * STEPS + i]
        old_old[a, b] = old_old[b, a] = spread[STEPS * STEPS + len(PAIRS) + i]
    turned = [
        [
            sum(old_old[j, i] * proj[i][k] for i in range(STEPS)) - 2.0 * proj[j][k]
            for k in range(STEPS)
        ]
        for j in range(STEPS)
    ]
    gram = {
        (a, b): new_new[a, b] + sum(proj[j][a] * turned[j][b] for j in range(STEPS))
        for a, b in PAIRS
    }
    lower, inverse = {}, []
    for b in range(STEPS):
        for a in range(b, STEPS):
            value = gram[b, a]
            for c in range(b):
                value = value - lower[a, c] * lower[b, c]
            if a == b:
                inverse.append(lax.rsqrt(value))
                lower[a, b] = value * inverse[b]
            else:
                lower[a, b] = value * inverse[b]
    lane, sub = lane_index(), row_index()
    proj_tile = jnp.zeros((8, LANES), jnp.float32)
    factor_tile = proj_tile
    for a in range(STEPS):
        for b in range(STEPS):
            here = (sub == a) & (lane == b)
            proj_tile = jnp.where(here, proj[a][b], proj_tile)
            if b >= a:
                factor_tile = jnp.where(here, lower[b, a], factor_tile)
    proj_out[...] = proj_tile[:STEPS, :STEPS]
    factor_out[...] = factor_tile[:STEPS, :STEPS]

    def field(f, carry):
        for x in range(2 * STEPS):
            old = [basis[m, f, x] for m in range(STEPS)]
            made = []
            for k in range(STEPS):
                value = krylov[k, f, x]
                for m in range(STEPS):
                    value = value - proj[m][k] * old[m]
                for c in range(k):
                    value = value - lower[k, c] * made[c]
                made.append(value * inverse[k])
                new_out[k, f, x] = made[k]
        return carry

    lax.fori_loop(0, fields, field, 0)


def far(*arrays):
    return [pltpu.with_memory_space_constraint(a, pltpu.HBM) for a in arrays]


def swaps(size, first):
    pairs = [(i, (i + 1) % size) for i in range(first, size, 2)]
    return pairs + [(j, i) for i, j in pairs]


def ring(axes, size):
    up = [(i, (i + 1) % size) for i in range(size)]
    down = [(j, i) for i, j in up]
    return lambda v: lax.ppermute(v, axes, up), lambda v: lax.ppermute(v, axes, down)


def shape_of(*dims):
    return jax.ShapeDtypeStruct(dims, jnp.float32)


def kept(*dims):
    return pltpu.VMEM(dims, jnp.float32)


def near(*arrays):
    return [pltpu.with_memory_space_constraint(a, pltpu.VMEM) for a in arrays]


def on_device(sizes, basis, coeffs, mixing_matrix, base_speed, span_speed, polymer_gain):
    outer, inner, span = sizes
    count, fields, nx, ny, nz = basis.shape
    total = float(basis[0].size * outer * inner * span)
    everything = fields + EXTRA
    slab = kept(everything, STEPS, ny, nz)
    vectors = (count, fields, nx, ny, nz)
    params = pltpu.CompilerParams(vmem_limit_bytes=16 * 2**20)
    cross, chip, held = pl.pallas_call(
        start_kernel,
        out_shape=(slab, slab, kept(*vectors)),
        in_specs=[HBM] * 5,
        out_specs=(VMEM,) * 3,
        scratch_shapes=[
            pltpu.SMEM((count,), jnp.float32),
            pltpu.SemaphoreType.DMA(()),
            pltpu.SemaphoreType.DMA((2, count)),
            pltpu.SemaphoreType.DMA((EXTRA, 2)),
        ],
        compiler_params=params,
        name="start",
    )(*far(coeffs, basis, base_speed, span_speed, polymer_gain))
    stream = ("outer", "inner")
    from_cross = lax.ppermute(cross, stream, swaps(outer * inner, 1))
    from_chip = lax.ppermute(chip, stream, swaps(outer * inner, 0))
    own = pl.pallas_call(
        own_edges_kernel,
        out_shape=kept(everything, ny, nz),
        in_specs=[VMEM] * 2,
        out_specs=VMEM,
        compiler_params=params,
        name="own_edges",
    )(*near(cross, chip))
    halves = kept((everything + 1) // 2, ny, nz)
    packed, to_right, to_left = pl.pallas_call(
        edges_kernel,
        out_shape=(kept(everything, ny, nz), halves, halves),
        in_specs=[VMEM] * 3,
        out_specs=(VMEM,) * 3,
        compiler_params=params,
        name="edges",
    )(*near(from_cross, from_chip, own))
    up, down = ring("span", span)
    from_left, from_right = up(to_right), down(to_left)
    made, coefs, splat, old_sums = pl.pallas_call(
        first_kernel,
        out_shape=(
            kept(fields, 4 * STEPS, ny, nz),
            kept(EXTRA, 4 * STEPS, ny, nz),
            kept(fields * fields, ny, nz),
            kept(len(PAIRS), ny, nz),
        ),
        in_specs=[SMEM] + [VMEM] * 5,
        out_specs=(VMEM,) * 4,
        scratch_shapes=[pltpu.VMEM((everything, 4 * STEPS, ny, nz), jnp.float32)],
        compiler_params=params,
        name="first",
    )(mixing_matrix, *near(from_cross, cross, chip, from_chip, held))
    krylov, sums = pl.pallas_call(
        krylov_kernel,
        out_shape=(kept(*vectors), kept(inner, 1, nz)),
        in_specs=[VMEM] * 8,
        out_specs=(VMEM,) * 2,
        scratch_shapes=[
            pltpu.VMEM((2, fields, 2 * STEPS, ny, nz), jnp.float32),
            pltpu.VMEM((2, everything, 2, ny, nz), jnp.float32),
            pltpu.VMEM((fields, ny, nz), jnp.float32),
        ],
        compiler_params=params,
        name="krylov",
    )(*near(splat, packed, from_left, from_right, made, coefs, held, old_sums))
    sums = lax.all_to_all(sums, "inner", 0, 0, tiled=True)
    sums = jnp.broadcast_to(jnp.sum(sums, axis=0, keepdims=True), (outer * span, 1, nz))
    sums = lax.all_to_all(sums, ("outer", "span"), 0, 0, tiled=True)
    return pl.pallas_call(
        functools.partial(finish_kernel, total),
        out_shape=(shape_of(count, STEPS), shape_of(STEPS, STEPS), shape_of(*vectors)),
        in_specs=[VMEM] * 3,
        out_specs=(VMEM,) * 3,
        compiler_params=params,
        name="finish",
    )(*near(sums, krylov, held))


def solution(mesh):
    stream, span = mesh.shape["stream"], mesh.shape["span"]
    inner = 1
    while inner * inner < stream * span and stream % (2 * inner) == 0:
        inner *= 2
    outer = stream // inner
    split = Mesh(np.asarray(mesh.devices).reshape(outer, inner, span), ("outer", "inner", "span"))
    field = P(("outer", "inner"), None, "span")
    vectors = P(None, None, ("outer", "inner"), None, "span")
    return jax.shard_map(
        functools.partial(on_device, (outer, inner, span)),
        mesh=split,
        in_specs=(vectors, P(), P(), field, field, field),
        out_specs=(P(), P(), vectors),
        check_vma=False,
    )
```

```python
import functools

import jax
import jax.numpy as jnp
import numpy as np
from jax import lax
from jax.experimental import pallas as pl
from jax.experimental.pallas import tpu as pltpu
from jax.sharding import Mesh
from jax.sharding import PartitionSpec as P

STEPS = 4
LANES = 128
EXTRA = 3
VMEM = pl.BlockSpec(memory_space=pltpu.VMEM)
SMEM = pl.BlockSpec(memory_space=pltpu.SMEM)
HBM = pl.BlockSpec(memory_space=pltpu.HBM)
PAIRS = [(a, b) for a in range(STEPS) for b in range(a, STEPS)]


def lane_index():
    return lax.broadcasted_iota(jnp.int32, (8, LANES), 1)


def row_index():
    return lax.broadcasted_iota(jnp.int32, (8, LANES), 0)


def parity():
    return lax.axis_index("inner") % 2


def start_kernel(
    coeffs, basis, base_speed, span_speed, gain, cross, chip, held, weights, weight_sem, basis_sems, field_sems
):
    count, fields = basis.shape[0], basis.shape[1]
    half = fields // 2
    first_row = STEPS * parity()
    sides = ((cross, first_row), (chip, STEPS - first_row))
    weight_copy = pltpu.make_async_copy(coeffs, weights, weight_sem)
    weight_copy.start()
    waves = []
    for w in range(2):
        span = pl.ds(w * half, half)
        waves.append(
            [
                pltpu.make_async_copy(basis.at[m, span], held.at[m, span], basis_sems.at[w, m])
                for m in range(count)
            ]
        )
        for copy in waves[w]:
            copy.start()
    copies = []
    for e, ref in enumerate((base_speed, span_speed, gain)):
        for i, (out, row) in enumerate(sides):
            copies.append(
                pltpu.make_async_copy(
                    ref.at[pl.ds(row, STEPS)], out.at[fields + e], field_sems.at[e, i]
                )
            )
            copies[-1].start()
    weight_copy.wait()
    scale = [weights[m] for m in range(count)]

    def field(f, carry):
        for r in range(STEPS):
            for out, row in sides:
                value = scale[0] * held[0, f, row + r]
                for m in range(1, count):
                    value = value + scale[m] * held[m, f, row + r]
                out[f, r] = value
        return carry

    for w in range(2):
        for copy in waves[w]:
            copy.wait()
        lax.fori_loop(w * half, (w + 1) * half, field, 0)
    for copy in copies:
        copy.wait()


def pack(tiles, value):
    group = lane_index() // 8
    for r, tile in tiles:
        value = jnp.where(group == r, pltpu.roll(tile, 8 * r + 4, 1), value)
    return value


def prepare_kernel(mixing, cross, chip, held, own, splat, old_sums):
    fields, side = held.shape[1], STEPS * parity()
    blank = jnp.zeros((8, LANES), jnp.float32)
    for f in range(own.shape[0]):
        rows = [(STEPS + side + r, cross[f, r]) for r in range(STEPS)]
        rows += [(2 * STEPS - side + r, chip[f, r]) for r in range(STEPS)]
        own[f] = pack(rows, blank)
    for f in range(fields):
        for g in range(fields):
            splat[f * fields + g] = jnp.full((8, LANES), mixing[f, g], jnp.float32)

    def products(f, totals):
        totals = list(totals)
        for x in range(2 * STEPS):
            old = [held[m, f, x] for m in range(STEPS)]
            for i, (a, b) in enumerate(PAIRS):
                totals[i] = totals[i] + old[a] * old[b]
        return tuple(totals)

    for i, total in enumerate(lax.fori_loop(0, fields, products, (blank,) * len(PAIRS))):
        old_sums[i] = total


def edges_kernel(from_cross, from_chip, own, packed, to_right, to_left):
    side = 3 * STEPS * parity()
    made = []
    for f in range(own.shape[0]):
        rows = [(side + r, from_cross[f, r]) for r in range(STEPS)]
        rows += [(3 * STEPS - side + r, from_chip[f, r]) for r in range(STEPS)]
        made.append(pack(rows, own[f]))
        packed[f] = made[f]
    inner = lane_index() % 8 < 4
    for q in range(to_right.shape[0]):
        even, odd = made[2 * q], made[min(2 * q + 1, len(made) - 1)]
        to_right[q] = jnp.where(inner, even, pltpu.roll(odd, 4, 1))
        to_left[q] = jnp.where(inner, pltpu.roll(odd, LANES - 4, 1), even)


def speeds(base, span):
    half_x, half_z = 0.5 * base, 0.5 * span
    return 0.05 - half_x, 0.05 + half_x, 0.05 - half_z, 0.05 + half_z


def walls():
    sub = row_index()
    return (
        jnp.where(sub < 7, 0.05, 0.0).astype(jnp.float32),
        jnp.where(sub > 0, 0.05, 0.0).astype(jnp.float32),
    )


def stencil(splat, items, wall, store):
    fields = len(items[0][0])
    scales = [speeds(item[5], item[6]) for item in items]
    for f in range(fields):
        mixed = [None] * len(items)
        for g in range(fields):
            weight = splat[f * fields + g]
            for i, item in enumerate(items):
                part = weight * item[0][g]
                mixed[i] = part if g == 0 else mixed[i] + part
        for i, (values, x_up, x_down, z_up, z_down, _, _, gain) in enumerate(items):
            c_xu, c_xd, c_zu, c_zd = scales[i]
            v = values[f]
            near_x = c_xu * x_up(f) + c_xd * x_down(f)
            near_z = c_zu * z_up(f) + c_zd * z_down(f)
            near_y = wall[0] * pltpu.roll(v, 7, 0) + wall[1] * pltpu.roll(v, 1, 0)
            store(i, f, (near_x + near_z) + (near_y - 0.3 * v) + gain * mixed[i])


def alone_kernel(splat, from_cross, cross, chip, from_chip, made, slabs, outer_rows):
    fields, rows = cross.shape[0] - EXTRA, 4 * STEPS
    lane, wall = lane_index(), walls()
    side = STEPS * parity()
    for ref, row in (
        (from_cross, 3 * side),
        (cross, STEPS + side),
        (chip, 2 * STEPS - side),
        (from_chip, 3 * (STEPS - side)),
    ):
        slabs[:, pl.ds(row, STEPS)] = ref[...]

    def place(k, r):
        if k < 0:
            return slabs, r
        if STEPS <= r < 3 * STEPS:
            return made.at[k], r - STEPS
        return outer_rows.at[k % 2], r if r < STEPS else r - 2 * STEPS

    for k in range(STEPS):

        def tile(f, r):
            ref, at = place(k - 1, r)
            return ref[f, at]

        def item(r):
            values = [tile(f, r) for f in range(fields)]
            return (
                values,
                lambda f: tile(f, r + 1),
                lambda f: tile(f, r - 1),
                lambda f: jnp.where(lane == LANES - 1, 0.0, pltpu.roll(values[f], LANES - 1, 1)),
                lambda f: jnp.where(lane == 0, 0.0, pltpu.roll(values[f], 1, 1)),
                slabs[fields, r],
                slabs[fields + 1, r],
                slabs[fields + 2, r],
            )

        for r in range(k + 1, rows - k - 1, 2):

            def store(i, f, value):
                ref, at = place(k, r + i)
                ref[f, at] = value

            stencil(splat, [item(r), item(r + 1)], wall, store)


def krylov_kernel(
    splat, own, from_left, from_right, made, held, old_sums, krylov, sums, rim, change
):
    fields = held.shape[1]
    lane, wall = lane_index(), walls()
    place = lane % 8
    inner = place < 4
    for f in range(fields + EXTRA):
        mine, left, right = own[f], from_left[f // 2], from_right[f // 2]
        if f % 2:
            left, right = pltpu.roll(left, LANES - 4, 1), pltpu.roll(right, 4, 1)
        rim[0, f, 0] = jnp.where(inner, left, mine)
        rim[0, f, 1] = jnp.where(inner, mine, right)

    _, _, c_zu, c_zd = speeds(own[fields], own[fields + 1])
    c_zu, c_zd = jnp.where(place == 3, c_zu, 0.0), jnp.where(place == 4, c_zd, 0.0)
    for f in range(fields):
        change[0, f] = c_zu * pltpu.roll(rim[0, f, 1], LANES - 1, 1) + c_zd * pltpu.roll(rim[0, f, 0], 1, 1)

    for k in range(STEPS):

        def edge(e):
            values = [rim[k, f, e] for f in range(fields)]
            return (
                values,
                lambda f: pltpu.roll(values[f], LANES - 8, 1),
                lambda f: pltpu.roll(values[f], 8, 1),
                lambda f: pltpu.roll(values[f], LANES - 1, 1),
                lambda f: pltpu.roll(values[f], 1, 1),
                rim[0, fields, e],
                rim[0, fields + 1, e],
                rim[0, fields + 2, e],
            )

        def inside():
            values = [change[k - 1, f] for f in range(fields)]
            return (
                values,
                lambda f: pltpu.roll(values[f], LANES - 8, 1),
                lambda f: pltpu.roll(values[f], 8, 1),
                lambda f: pltpu.roll(jnp.where(place == 4, rim[k, f, 1], values[f]), LANES - 1, 1),
                lambda f: pltpu.roll(jnp.where(place == 3, rim[k, f, 0], values[f]), 1, 1),
                own[fields],
                own[fields + 1],
                own[fields + 2],
            )

        items = [edge(0), edge(1)] if k + 1 < STEPS else []
        edges = len(items)
        if k:
            items.append(inside())

        def store(i, f, value):
            if i < edges:
                rim[k + 1, f, i] = value
            else:
                change[k, f] = value

        stencil(splat, items, wall, store)

    face = (lane < STEPS) | (lane >= LANES - STEPS)

    def products(f, totals):
        totals = list(totals)
        for x in range(2 * STEPS):
            new = []
            for k in range(STEPS):
                turned = pltpu.roll(change[k, f], LANES - (8 * (x + STEPS) + 4), 1)
                new.append(made[k, f, x] + jnp.where(face, turned, 0.0))
                krylov[k, f, x] = new[k]
            old = [held[m, f, x] for m in range(STEPS)]
            i = 0
            for a in range(STEPS):
                for b in range(STEPS):
                    totals[i] = totals[i] + old[a] * new[b]
                    i += 1
            for a, b in PAIRS:
                totals[i] = totals[i] + new[a] * new[b]
                i += 1
        return tuple(totals)

    zero = jnp.zeros((8, LANES), jnp.float32)
    totals = (zero,) * (STEPS * STEPS + len(PAIRS))
    for f in range(fields):
        totals = products(f, totals)
    totals = list(totals) + [old_sums[i] for i in range(len(PAIRS))]
    lines = [jnp.sum(t, axis=0, keepdims=True) for t in totals]
    lines.append(jnp.zeros((LANES - len(lines), LANES), jnp.float32))
    table = jnp.concatenate(lines, axis=0)
    row_sums = lax.dot_general(
        jnp.ones((8, LANES), jnp.float32),
        table,
        (((1,), (1,)), ((), ())),
        precision=lax.Precision.HIGHEST,
        preferred_element_type=jnp.float32,
    )
    for i in range(sums.shape[0]):
        sums[i] = row_sums[0:1]


def finish_kernel(total, parts, krylov, basis, proj_out, factor_out, new_out):
    fields = basis.shape[1]
    line = parts[0]
    for i in range(1, parts.shape[0]):
        line = line + parts[i]
    line = jnp.broadcast_to(line / total, (8, LANES))
    spread = [
        jnp.broadcast_to(line[:, i : i + 1], (8, LANES))
        for i in range(STEPS * STEPS + 2 * len(PAIRS))
    ]
    proj = [[spread[a * STEPS + b] for b in range(STEPS)] for a in range(STEPS)]
    new_new, old_old = {}, {}
    for i, (a, b) in enumerate(PAIRS):
        new_new[a, b] = spread[STEPS * STEPS + i]
        old_old[a, b] = old_old[b, a] = spread[STEPS * STEPS + len(PAIRS) + i]
    turned = [
        [
            sum(old_old[j, i] * proj[i][k] for i in range(STEPS)) - 2.0 * proj[j][k]
            for k in range(STEPS)
        ]
        for j in range(STEPS)
    ]
    gram = {
        (a, b): new_new[a, b] + sum(proj[j][a] * turned[j][b] for j in range(STEPS))
        for a, b in PAIRS
    }
    lower, inverse = {}, []
    for b in range(STEPS):
        for a in range(b, STEPS):
            value = gram[b, a]
            for c in range(b):
                value = value - lower[a, c] * lower[b, c]
            if a == b:
                inverse.append(lax.rsqrt(value))
                lower[a, b] = value * inverse[b]
            else:
                lower[a, b] = value * inverse[b]
    lane, sub = lane_index(), row_index()
    proj_tile = jnp.zeros((8, LANES), jnp.float32)
    factor_tile = proj_tile
    for a in range(STEPS):
        for b in range(STEPS):
            here = (sub == a) & (lane == b)
            proj_tile = jnp.where(here, proj[a][b], proj_tile)
            if b >= a:
                factor_tile = jnp.where(here, lower[b, a], factor_tile)
    proj_out[...] = proj_tile[:STEPS, :STEPS]
    factor_out[...] = factor_tile[:STEPS, :STEPS]

    def field(f, carry):
        for x in range(2 * STEPS):
            old = [basis[m, f, x] for m in range(STEPS)]
            made = []
            for k in range(STEPS):
                value = krylov[k, f, x]
                for m in range(STEPS):
                    value = value - proj[m][k] * old[m]
                for c in range(k):
                    value = value - lower[k, c] * made[c]
                made.append(value * inverse[k])
                new_out[k, f, x] = made[k]
        return carry

    lax.fori_loop(0, fields, field, 0)


def far(*arrays):
    return [pltpu.with_memory_space_constraint(a, pltpu.HBM) for a in arrays]


def swaps(size, first):
    pairs = [(i, (i + 1) % size) for i in range(first, size, 2)]
    return pairs + [(j, i) for i, j in pairs]


def ring(axes, size):
    up = [(i, (i + 1) % size) for i in range(size)]
    down = [(j, i) for i, j in up]
    return lambda v: lax.ppermute(v, axes, up), lambda v: lax.ppermute(v, axes, down)


def shape_of(*dims):
    return jax.ShapeDtypeStruct(dims, jnp.float32)


def kept(*dims):
    return pltpu.VMEM(dims, jnp.float32)


def near(*arrays):
    return [pltpu.with_memory_space_constraint(a, pltpu.VMEM) for a in arrays]


def on_device(sizes, basis, coeffs, mixing_matrix, base_speed, span_speed, polymer_gain):
    outer, inner, span = sizes
    count, fields, nx, ny, nz = basis.shape
    total = float(basis[0].size * outer * inner * span)
    everything = fields + EXTRA
    slab = kept(everything, STEPS, ny, nz)
    vectors = (count, fields, nx, ny, nz)
    params = pltpu.CompilerParams(vmem_limit_bytes=16 * 2**20)
    cross, chip, held = pl.pallas_call(
        start_kernel,
        out_shape=(slab, slab, kept(*vectors)),
        in_specs=[HBM] * 5,
        out_specs=(VMEM,) * 3,
        scratch_shapes=[
            pltpu.SMEM((count,), jnp.float32),
            pltpu.SemaphoreType.DMA(()),
            pltpu.SemaphoreType.DMA((2, count)),
            pltpu.SemaphoreType.DMA((EXTRA, 2)),
        ],
        compiler_params=params,
        name="start",
    )(*far(coeffs, basis, base_speed, span_speed, polymer_gain))
    stream = ("outer", "inner")
    from_cross = lax.ppermute(cross, stream, swaps(outer * inner, 1))
    from_chip = lax.ppermute(chip, stream, swaps(outer * inner, 0))
    own, splat, old_sums = pl.pallas_call(
        prepare_kernel,
        out_shape=(
            kept(everything, ny, nz),
            kept(fields * fields, ny, nz),
            kept(len(PAIRS), ny, nz),
        ),
        in_specs=[SMEM] + [VMEM] * 3,
        out_specs=(VMEM,) * 3,
        compiler_params=params,
        name="prepare",
    )(mixing_matrix, *near(cross, chip, held))
    halves = kept((everything + 1) // 2, ny, nz)
    packed, to_right, to_left = pl.pallas_call(
        edges_kernel,
        out_shape=(kept(everything, ny, nz), halves, halves),
        in_specs=[VMEM] * 3,
        out_specs=(VMEM,) * 3,
        compiler_params=params,
        name="edges",
    )(*near(from_cross, from_chip, own))
    up, down = ring("span", span)
    from_left, from_right = up(to_right), down(to_left)
    made = pl.pallas_call(
        alone_kernel,
        out_shape=kept(*vectors),
        in_specs=[VMEM] * 5,
        out_specs=VMEM,
        scratch_shapes=[
            pltpu.VMEM((everything, 4 * STEPS, ny, nz), jnp.float32),
            pltpu.VMEM((2, fields, 2 * STEPS, ny, nz), jnp.float32),
        ],
        compiler_params=params,
        name="alone",
    )(*near(splat, from_cross, cross, chip, from_chip))
    krylov, sums = pl.pallas_call(
        krylov_kernel,
        out_shape=(kept(*vectors), kept(inner, 1, nz)),
        in_specs=[VMEM] * 7,
        out_specs=(VMEM,) * 2,
        scratch_shapes=[
            pltpu.VMEM((STEPS, everything, 2, ny, nz), jnp.float32),
            pltpu.VMEM((STEPS, fields, ny, nz), jnp.float32),
        ],
        compiler_params=params,
        name="krylov",
    )(*near(splat, packed, from_left, from_right, made, held, old_sums))
    sums = lax.all_to_all(sums, "inner", 0, 0, tiled=True)
    sums = jnp.broadcast_to(jnp.sum(sums, axis=0, keepdims=True), (outer * span, 1, nz))
    sums = lax.all_to_all(sums, ("outer", "span"), 0, 0, tiled=True)
    return pl.pallas_call(
        functools.partial(finish_kernel, total),
        out_shape=(shape_of(count, STEPS), shape_of(STEPS, STEPS), shape_of(*vectors)),
        in_specs=[VMEM] * 3,
        out_specs=(VMEM,) * 3,
        compiler_params=params,
        name="finish",
    )(*near(sums, krylov, held))


def solution(mesh):
    stream, span = mesh.shape["stream"], mesh.shape["span"]
    inner = 1
    while inner * inner < stream * span and stream % (2 * inner) == 0:
        inner *= 2
    outer = stream // inner
    split = Mesh(np.asarray(mesh.devices).reshape(outer, inner, span), ("outer", "inner", "span"))
    field = P(("outer", "inner"), None, "span")
    vectors = P(None, None, ("outer", "inner"), None, "span")
    return jax.shard_map(
        functools.partial(on_device, (outer, inner, span)),
        mesh=split,
        in_specs=(vectors, P(), P(), field, field, field),
        out_specs=(P(), P(), vectors),
        check_vma=False,
    )
```

```python
import functools
import math

import jax
import jax.numpy as jnp
import numpy as np
from jax import lax
from jax.experimental import pallas as pl
from jax.experimental.pallas import tpu as pltpu
from jax.sharding import Mesh
from jax.sharding import PartitionSpec as P

STEPS = 4
LANES = 128
EXTRA = 3
VMEM = pl.BlockSpec(memory_space=pltpu.VMEM)
SMEM = pl.BlockSpec(memory_space=pltpu.SMEM)
HBM = pl.BlockSpec(memory_space=pltpu.HBM)
PAIRS = [(a, b) for a in range(STEPS) for b in range(a, STEPS)]


def lane_index():
    return lax.broadcasted_iota(jnp.int32, (8, LANES), 1)


def row_index():
    return lax.broadcasted_iota(jnp.int32, (8, LANES), 0)


def parity():
    return lax.axis_index("inner") % 2


def start_kernel(
    coeffs, basis, base_speed, span_speed, gain, cross, chip, held, weights, weight_sem, basis_sems, field_sems
):
    count, fields = basis.shape[0], basis.shape[1]
    half = fields // 2
    first_row = STEPS * parity()
    sides = ((cross, first_row), (chip, STEPS - first_row))
    weight_copy = pltpu.make_async_copy(coeffs, weights, weight_sem)
    weight_copy.start()
    waves = []
    for w in range(2):
        span = pl.ds(w * half, half)
        waves.append(
            [
                pltpu.make_async_copy(basis.at[m, span], held.at[m, span], basis_sems.at[w, m])
                for m in range(count)
            ]
        )
        for copy in waves[w]:
            copy.start()
    copies = []
    for e, ref in enumerate((base_speed, span_speed, gain)):
        for i, (out, row) in enumerate(sides):
            copies.append(
                pltpu.make_async_copy(
                    ref.at[pl.ds(row, STEPS)], out.at[fields + e], field_sems.at[e, i]
                )
            )
            copies[-1].start()
    weight_copy.wait()
    scale = [weights[m] for m in range(count)]

    def field(f, carry):
        for r in range(STEPS):
            for out, row in sides:
                value = scale[0] * held[0, f, row + r]
                for m in range(1, count):
                    value = value + scale[m] * held[m, f, row + r]
                out[f, r] = value
        return carry

    for w in range(2):
        for copy in waves[w]:
            copy.wait()
        lax.fori_loop(w * half, (w + 1) * half, field, 0)
    for copy in copies:
        copy.wait()


def pack(tiles, value):
    group = lane_index() // 8
    for r, tile in tiles:
        value = jnp.where(group == r, pltpu.roll(tile, 8 * r + 4, 1), value)
    return value


def edges_kernel(from_cross, from_chip, own, packed, to_right, to_left):
    side = 3 * STEPS * parity()
    made = []
    for f in range(own.shape[0]):
        rows = [(side + r, from_cross[f, r]) for r in range(STEPS)]
        rows += [(3 * STEPS - side + r, from_chip[f, r]) for r in range(STEPS)]
        made.append(pack(rows, own[f]))
        packed[f] = made[f]
    inner = lane_index() % 8 < 4
    for q in range(to_right.shape[0]):
        even, odd = made[2 * q], made[min(2 * q + 1, len(made) - 1)]
        to_right[q] = jnp.where(inner, even, pltpu.roll(odd, 4, 1))
        to_left[q] = jnp.where(inner, pltpu.roll(odd, LANES - 4, 1), even)


def speeds(base, span):
    half_x, half_z = 0.5 * base, 0.5 * span
    return 0.05 - half_x, 0.05 + half_x, 0.05 - half_z, 0.05 + half_z


def walls():
    sub = row_index()
    return (
        jnp.where(sub < 7, 0.05, 0.0).astype(jnp.float32),
        jnp.where(sub > 0, 0.05, 0.0).astype(jnp.float32),
    )


def stencil(splat, items, wall, store):
    fields = len(items[0][0])
    scales = [speeds(item[5], item[6]) for item in items]
    for f in range(fields):
        mixed = [None] * len(items)
        for g in range(fields):
            weight = splat[f * fields + g]
            for i, item in enumerate(items):
                part = weight * item[0][g]
                mixed[i] = part if g == 0 else mixed[i] + part
        for i, (values, x_up, x_down, z_up, z_down, _, _, gain) in enumerate(items):
            c_xu, c_xd, c_zu, c_zd = scales[i]
            v = values[f]
            near_x = c_xu * x_up(f) + c_xd * x_down(f)
            near_z = c_zu * z_up(f) + c_zd * z_down(f)
            near_y = wall[0] * pltpu.roll(v, 7, 0) + wall[1] * pltpu.roll(v, 1, 0)
            store(i, f, (near_x + near_z) + (near_y - 0.3 * v) + gain * mixed[i])


def advance(splat, tile, coef, rows, put):
    fields, lane, wall = math.isqrt(splat.shape[0]), lane_index(), walls()

    def item(r):
        values = [tile(f, r) for f in range(fields)]
        return (
            values,
            lambda f: tile(f, r + 1),
            lambda f: tile(f, r - 1),
            lambda f: jnp.where(lane == LANES - 1, 0.0, pltpu.roll(values[f], LANES - 1, 1)),
            lambda f: jnp.where(lane == 0, 0.0, pltpu.roll(values[f], 1, 1)),
            coef(0, r),
            coef(1, r),
            coef(2, r),
        )

    for pair in zip(rows[::2], rows[1::2]):

        def store(i, f, value):
            put(f, pair[i], value)

        stencil(splat, [item(r) for r in pair], wall, store)


def prepare_kernel(mixing, cross, chip, held, own, splat, old_sums, made, slabs):
    fields, side = held.shape[1], STEPS * parity()
    blank = jnp.zeros((8, LANES), jnp.float32)
    for f in range(own.shape[0]):
        rows = [(STEPS + side + r, cross[f, r]) for r in range(STEPS)]
        rows += [(2 * STEPS - side + r, chip[f, r]) for r in range(STEPS)]
        own[f] = pack(rows, blank)
    for f in range(fields):
        for g in range(fields):
            splat[f * fields + g] = jnp.full((8, LANES), mixing[f, g], jnp.float32)
    slabs[:, pl.ds(side, STEPS)] = cross[...]
    slabs[:, pl.ds(STEPS - side, STEPS)] = chip[...]
    for k in range(STEPS - 1):

        def tile(f, r):
            return made[k - 1, f, r] if k else slabs[f, r]

        def store(f, r, value):
            made[k, f, r] = value

        rows = list(range(k + 1, 2 * STEPS - k - 1))
        advance(splat, tile, lambda e, r: slabs[fields + e, r], rows, store)

    def products(f, totals):
        totals = list(totals)
        for x in range(2 * STEPS):
            old = [held[m, f, x] for m in range(STEPS)]
            for i, (a, b) in enumerate(PAIRS):
                totals[i] = totals[i] + old[a] * old[b]
        return tuple(totals)

    for i, total in enumerate(lax.fori_loop(0, fields, products, (blank,) * len(PAIRS))):
        old_sums[i] = total


def alone_kernel(splat, from_cross, cross, chip, from_chip, ahead, made, slabs, outer_rows):
    fields, rows = cross.shape[0] - EXTRA, 4 * STEPS
    side = STEPS * parity()
    for ref, row in (
        (from_cross, 3 * side),
        (cross, STEPS + side),
        (chip, 2 * STEPS - side),
        (from_chip, 3 * (STEPS - side)),
    ):
        slabs[:, pl.ds(row, STEPS)] = ref[...]

    def done(k, r):
        return STEPS + k < r < 3 * STEPS - k - 1

    for k in range(STEPS):

        def tile(f, r):
            if k == 0:
                return slabs[f, r]
            if STEPS <= r < 3 * STEPS:
                return (ahead if done(k - 1, r) else made)[k - 1, f, r - STEPS]
            return outer_rows[(k - 1) % 2, f, r if r < STEPS else r - 2 * STEPS]

        def put(f, r, value):
            if STEPS <= r < 3 * STEPS:
                made[k, f, r - STEPS] = value
            else:
                outer_rows[k % 2, f, r if r < STEPS else r - 2 * STEPS] = value

        left = [r for r in range(k + 1, rows - k - 1) if not done(k, r)]
        advance(splat, tile, lambda e, r: slabs[fields + e, r], left, put)


def krylov_kernel(
    splat, own, from_left, from_right, made, held, old_sums, krylov, sums, rim, change
):
    fields = held.shape[1]
    lane, wall = lane_index(), walls()
    place = lane % 8
    inner = place < 4
    for f in range(fields + EXTRA):
        mine, left, right = own[f], from_left[f // 2], from_right[f // 2]
        if f % 2:
            left, right = pltpu.roll(left, LANES - 4, 1), pltpu.roll(right, 4, 1)
        rim[0, f, 0] = jnp.where(inner, left, mine)
        rim[0, f, 1] = jnp.where(inner, mine, right)

    _, _, c_zu, c_zd = speeds(own[fields], own[fields + 1])
    c_zu, c_zd = jnp.where(place == 3, c_zu, 0.0), jnp.where(place == 4, c_zd, 0.0)
    for f in range(fields):
        change[0, f] = c_zu * pltpu.roll(rim[0, f, 1], LANES - 1, 1) + c_zd * pltpu.roll(rim[0, f, 0], 1, 1)

    for k in range(STEPS):

        def edge(e):
            values = [rim[k, f, e] for f in range(fields)]
            return (
                values,
                lambda f: pltpu.roll(values[f], LANES - 8, 1),
                lambda f: pltpu.roll(values[f], 8, 1),
                lambda f: pltpu.roll(values[f], LANES - 1, 1),
                lambda f: pltpu.roll(values[f], 1, 1),
                rim[0, fields, e],
                rim[0, fields + 1, e],
                rim[0, fields + 2, e],
            )

        def inside():
            values = [change[k - 1, f] for f in range(fields)]
            return (
                values,
                lambda f: pltpu.roll(values[f], LANES - 8, 1),
                lambda f: pltpu.roll(values[f], 8, 1),
                lambda f: pltpu.roll(jnp.where(place == 4, rim[k, f, 1], values[f]), LANES - 1, 1),
                lambda f: pltpu.roll(jnp.where(place == 3, rim[k, f, 0], values[f]), 1, 1),
                own[fields],
                own[fields + 1],
                own[fields + 2],
            )

        items = [edge(0), edge(1)] if k + 1 < STEPS else []
        edges = len(items)
        if k:
            items.append(inside())

        def store(i, f, value):
            if i < edges:
                rim[k + 1, f, i] = value
            else:
                change[k, f] = value

        stencil(splat, items, wall, store)

    face = (lane < STEPS) | (lane >= LANES - STEPS)

    def products(f, totals):
        totals = list(totals)
        for x in range(2 * STEPS):
            new = []
            for k in range(STEPS):
                turned = pltpu.roll(change[k, f], LANES - (8 * (x + STEPS) + 4), 1)
                new.append(made[k, f, x] + jnp.where(face, turned, 0.0))
                krylov[k, f, x] = new[k]
            old = [held[m, f, x] for m in range(STEPS)]
            i = 0
            for a in range(STEPS):
                for b in range(STEPS):
                    totals[i] = totals[i] + old[a] * new[b]
                    i += 1
            for a, b in PAIRS:
                totals[i] = totals[i] + new[a] * new[b]
                i += 1
        return tuple(totals)

    zero = jnp.zeros((8, LANES), jnp.float32)
    totals = (zero,) * (STEPS * STEPS + len(PAIRS))
    for f in range(fields):
        totals = products(f, totals)
    totals = list(totals) + [old_sums[i] for i in range(len(PAIRS))]
    lines = [jnp.sum(t, axis=0, keepdims=True) for t in totals]
    lines.append(jnp.zeros((LANES - len(lines), LANES), jnp.float32))
    table = jnp.concatenate(lines, axis=0)
    row_sums = lax.dot_general(
        jnp.ones((8, LANES), jnp.float32),
        table,
        (((1,), (1,)), ((), ())),
        precision=lax.Precision.HIGHEST,
        preferred_element_type=jnp.float32,
    )
    for i in range(sums.shape[0]):
        sums[i] = row_sums[0:1]


def finish_kernel(total, parts, krylov, basis, proj_out, factor_out, new_out):
    fields = basis.shape[1]
    line = parts[0]
    for i in range(1, parts.shape[0]):
        line = line + parts[i]
    line = jnp.broadcast_to(line / total, (8, LANES))
    spread = [
        jnp.broadcast_to(line[:, i : i + 1], (8, LANES))
        for i in range(STEPS * STEPS + 2 * len(PAIRS))
    ]
    proj = [[spread[a * STEPS + b] for b in range(STEPS)] for a in range(STEPS)]
    new_new, old_old = {}, {}
    for i, (a, b) in enumerate(PAIRS):
        new_new[a, b] = spread[STEPS * STEPS + i]
        old_old[a, b] = old_old[b, a] = spread[STEPS * STEPS + len(PAIRS) + i]
    turned = [
        [
            sum(old_old[j, i] * proj[i][k] for i in range(STEPS)) - 2.0 * proj[j][k]
            for k in range(STEPS)
        ]
        for j in range(STEPS)
    ]
    gram = {
        (a, b): new_new[a, b] + sum(proj[j][a] * turned[j][b] for j in range(STEPS))
        for a, b in PAIRS
    }
    lower, inverse = {}, []
    for b in range(STEPS):
        for a in range(b, STEPS):
            value = gram[b, a]
            for c in range(b):
                value = value - lower[a, c] * lower[b, c]
            if a == b:
                inverse.append(lax.rsqrt(value))
                lower[a, b] = value * inverse[b]
            else:
                lower[a, b] = value * inverse[b]
    lane, sub = lane_index(), row_index()
    proj_tile = jnp.zeros((8, LANES), jnp.float32)
    factor_tile = proj_tile
    for a in range(STEPS):
        for b in range(STEPS):
            here = (sub == a) & (lane == b)
            proj_tile = jnp.where(here, proj[a][b], proj_tile)
            if b >= a:
                factor_tile = jnp.where(here, lower[b, a], factor_tile)
    proj_out[...] = proj_tile[:STEPS, :STEPS]
    factor_out[...] = factor_tile[:STEPS, :STEPS]

    def field(f, carry):
        for x in range(2 * STEPS):
            old = [basis[m, f, x] for m in range(STEPS)]
            made = []
            for k in range(STEPS):
                value = krylov[k, f, x]
                for m in range(STEPS):
                    value = value - proj[m][k] * old[m]
                for c in range(k):
                    value = value - lower[k, c] * made[c]
                made.append(value * inverse[k])
                new_out[k, f, x] = made[k]
        return carry

    lax.fori_loop(0, fields, field, 0)


def far(*arrays):
    return [pltpu.with_memory_space_constraint(a, pltpu.HBM) for a in arrays]


def swaps(size, first):
    pairs = [(i, (i + 1) % size) for i in range(first, size, 2)]
    return pairs + [(j, i) for i, j in pairs]


def ring(axes, size):
    up = [(i, (i + 1) % size) for i in range(size)]
    down = [(j, i) for i, j in up]
    return lambda v: lax.ppermute(v, axes, up), lambda v: lax.ppermute(v, axes, down)


def shape_of(*dims):
    return jax.ShapeDtypeStruct(dims, jnp.float32)


def kept(*dims):
    return pltpu.VMEM(dims, jnp.float32)


def near(*arrays):
    return [pltpu.with_memory_space_constraint(a, pltpu.VMEM) for a in arrays]


def on_device(sizes, basis, coeffs, mixing_matrix, base_speed, span_speed, polymer_gain):
    outer, inner, span = sizes
    count, fields, nx, ny, nz = basis.shape
    total = float(basis[0].size * outer * inner * span)
    everything = fields + EXTRA
    slab = kept(everything, STEPS, ny, nz)
    vectors = (count, fields, nx, ny, nz)
    params = pltpu.CompilerParams(vmem_limit_bytes=16 * 2**20)
    cross, chip, held = pl.pallas_call(
        start_kernel,
        out_shape=(slab, slab, kept(*vectors)),
        in_specs=[HBM] * 5,
        out_specs=(VMEM,) * 3,
        scratch_shapes=[
            pltpu.SMEM((count,), jnp.float32),
            pltpu.SemaphoreType.DMA(()),
            pltpu.SemaphoreType.DMA((2, count)),
            pltpu.SemaphoreType.DMA((EXTRA, 2)),
        ],
        compiler_params=params,
        name="start",
    )(*far(coeffs, basis, base_speed, span_speed, polymer_gain))
    stream = ("outer", "inner")
    from_cross = lax.ppermute(cross, stream, swaps(outer * inner, 1))
    from_chip = lax.ppermute(chip, stream, swaps(outer * inner, 0))
    own, splat, old_sums, ahead = pl.pallas_call(
        prepare_kernel,
        out_shape=(
            kept(everything, ny, nz),
            kept(fields * fields, ny, nz),
            kept(len(PAIRS), ny, nz),
            kept(*vectors),
        ),
        in_specs=[SMEM] + [VMEM] * 3,
        out_specs=(VMEM,) * 4,
        scratch_shapes=[pltpu.VMEM((everything, 2 * STEPS, ny, nz), jnp.float32)],
        compiler_params=params,
        name="prepare",
    )(mixing_matrix, *near(cross, chip, held))
    halves = kept((everything + 1) // 2, ny, nz)
    packed, to_right, to_left = pl.pallas_call(
        edges_kernel,
        out_shape=(kept(everything, ny, nz), halves, halves),
        in_specs=[VMEM] * 3,
        out_specs=(VMEM,) * 3,
        compiler_params=params,
        name="edges",
    )(*near(from_cross, from_chip, own))
    up, down = ring("span", span)
    from_left, from_right = up(to_right), down(to_left)
    made = pl.pallas_call(
        alone_kernel,
        out_shape=kept(*vectors),
        in_specs=[VMEM] * 6,
        out_specs=VMEM,
        input_output_aliases={5: 0},
        scratch_shapes=[
            pltpu.VMEM((everything, 4 * STEPS, ny, nz), jnp.float32),
            pltpu.VMEM((2, fields, 2 * STEPS, ny, nz), jnp.float32),
        ],
        compiler_params=params,
        name="alone",
    )(*near(splat, from_cross, cross, chip, from_chip, ahead))
    krylov, sums = pl.pallas_call(
        krylov_kernel,
        out_shape=(kept(*vectors), kept(inner, 1, nz)),
        in_specs=[VMEM] * 7,
        out_specs=(VMEM,) * 2,
        scratch_shapes=[
            pltpu.VMEM((STEPS, everything, 2, ny, nz), jnp.float32),
            pltpu.VMEM((STEPS, fields, ny, nz), jnp.float32),
        ],
        compiler_params=params,
        name="krylov",
    )(*near(splat, packed, from_left, from_right, made, held, old_sums))
    sums = lax.all_to_all(sums, "inner", 0, 0, tiled=True)
    sums = jnp.broadcast_to(jnp.sum(sums, axis=0, keepdims=True), (outer * span, 1, nz))
    sums = lax.all_to_all(sums, ("outer", "span"), 0, 0, tiled=True)
    return pl.pallas_call(
        functools.partial(finish_kernel, total),
        out_shape=(shape_of(count, STEPS), shape_of(STEPS, STEPS), shape_of(*vectors)),
        in_specs=[VMEM] * 3,
        out_specs=(VMEM,) * 3,
        compiler_params=params,
        name="finish",
    )(*near(sums, krylov, held))


def solution(mesh):
    stream, span = mesh.shape["stream"], mesh.shape["span"]
    inner = 1
    while inner * inner < stream * span and stream % (2 * inner) == 0:
        inner *= 2
    outer = stream // inner
    split = Mesh(np.asarray(mesh.devices).reshape(outer, inner, span), ("outer", "inner", "span"))
    field = P(("outer", "inner"), None, "span")
    vectors = P(None, None, ("outer", "inner"), None, "span")
    return jax.shard_map(
        functools.partial(on_device, (outer, inner, span)),
        mesh=split,
        in_specs=(vectors, P(), P(), field, field, field),
        out_specs=(P(), P(), vectors),
        check_vma=False,
    )
```

```python
import functools
import math

import jax
import jax.numpy as jnp
import numpy as np
from jax import lax
from jax.experimental import pallas as pl
from jax.experimental.pallas import tpu as pltpu
from jax.sharding import Mesh
from jax.sharding import PartitionSpec as P

STEPS = 4
LANES = 128
EXTRA = 3
VMEM = pl.BlockSpec(memory_space=pltpu.VMEM)
SMEM = pl.BlockSpec(memory_space=pltpu.SMEM)
HBM = pl.BlockSpec(memory_space=pltpu.HBM)
PAIRS = [(a, b) for a in range(STEPS) for b in range(a, STEPS)]


def lane_index():
    return lax.broadcasted_iota(jnp.int32, (8, LANES), 1)


def row_index():
    return lax.broadcasted_iota(jnp.int32, (8, LANES), 0)


def parity():
    return lax.axis_index("inner") % 2


def start_kernel(
    coeffs, basis, base_speed, span_speed, gain, cross, chip, held, weights, weight_sem, basis_sems, field_sems
):
    count, fields = basis.shape[0], basis.shape[1]
    half = fields // 2
    first_row = STEPS * parity()
    sides = ((cross, first_row), (chip, STEPS - first_row))
    weight_copy = pltpu.make_async_copy(coeffs, weights, weight_sem)
    weight_copy.start()
    waves = []
    for w in range(2):
        span = pl.ds(w * half, half)
        waves.append(
            [
                pltpu.make_async_copy(basis.at[m, span], held.at[m, span], basis_sems.at[w, m])
                for m in range(count)
            ]
        )
        for copy in waves[w]:
            copy.start()
    copies = []
    for e, ref in enumerate((base_speed, span_speed, gain)):
        for i, (out, row) in enumerate(sides):
            copies.append(
                pltpu.make_async_copy(
                    ref.at[pl.ds(row, STEPS)], out.at[fields + e], field_sems.at[e, i]
                )
            )
            copies[-1].start()
    weight_copy.wait()
    scale = [weights[m] for m in range(count)]

    def field(f, carry):
        for r in range(STEPS):
            for out, row in sides:
                value = scale[0] * held[0, f, row + r]
                for m in range(1, count):
                    value = value + scale[m] * held[m, f, row + r]
                out[f, r] = value
        return carry

    for w in range(2):
        for copy in waves[w]:
            copy.wait()
        lax.fori_loop(w * half, (w + 1) * half, field, 0)
    for copy in copies:
        copy.wait()


def pack(tiles, value):
    group = lane_index() // 8
    for r, tile in tiles:
        value = jnp.where(group == r, pltpu.roll(tile, 8 * r + 4, 1), value)
    return value


def edges_kernel(from_cross, from_chip, own, packed, to_right, to_left):
    side = 3 * STEPS * parity()
    made = []
    for f in range(own.shape[0]):
        rows = [(side + r, from_cross[f, r]) for r in range(STEPS)]
        rows += [(3 * STEPS - side + r, from_chip[f, r]) for r in range(STEPS)]
        made.append(pack(rows, own[f]))
        packed[f] = made[f]
    inner = lane_index() % 8 < 4
    for q in range(to_right.shape[0]):
        even, odd = made[2 * q], made[min(2 * q + 1, len(made) - 1)]
        to_right[q] = jnp.where(inner, even, pltpu.roll(odd, 4, 1))
        to_left[q] = jnp.where(inner, pltpu.roll(odd, LANES - 4, 1), even)


def speeds(base, span):
    half_x, half_z = 0.5 * base, 0.5 * span
    return 0.05 - half_x, 0.05 + half_x, 0.05 - half_z, 0.05 + half_z


def walls():
    sub = row_index()
    return (
        jnp.where(sub < 7, 0.05, 0.0).astype(jnp.float32),
        jnp.where(sub > 0, 0.05, 0.0).astype(jnp.float32),
    )


def stencil(splat, items, wall, store):
    fields = len(items[0][0])
    scales = [speeds(item[5], item[6]) for item in items]
    for f in range(fields):
        mixed = [None] * len(items)
        for g in range(fields):
            weight = splat[f * fields + g]
            for i, item in enumerate(items):
                part = weight * item[0][g]
                mixed[i] = part if g == 0 else mixed[i] + part
        for i, (values, x_up, x_down, z_up, z_down, _, _, gain) in enumerate(items):
            c_xu, c_xd, c_zu, c_zd = scales[i]
            v = values[f]
            near_x = c_xu * x_up(f) + c_xd * x_down(f)
            near_z = c_zu * z_up(f) + c_zd * z_down(f)
            near_y = wall[0] * pltpu.roll(v, 7, 0) + wall[1] * pltpu.roll(v, 1, 0)
            store(i, f, (near_x + near_z) + (near_y - 0.3 * v) + gain * mixed[i])


def advance(splat, tile, coef, rows, put):
    fields, lane, wall = math.isqrt(splat.shape[0]), lane_index(), walls()

    def item(r):
        values = [tile(f, r) for f in range(fields)]
        return (
            values,
            lambda f: tile(f, r + 1),
            lambda f: tile(f, r - 1),
            lambda f: jnp.where(lane == LANES - 1, 0.0, pltpu.roll(values[f], LANES - 1, 1)),
            lambda f: jnp.where(lane == 0, 0.0, pltpu.roll(values[f], 1, 1)),
            coef(0, r),
            coef(1, r),
            coef(2, r),
        )

    for pair in zip(rows[::2], rows[1::2]):

        def store(i, f, value):
            put(f, pair[i], value)

        stencil(splat, [item(r) for r in pair], wall, store)


def prepare_kernel(mixing, cross, chip, held, own, splat, old_sums, made, slabs):
    fields, side = held.shape[1], STEPS * parity()
    blank = jnp.zeros((8, LANES), jnp.float32)
    for f in range(own.shape[0]):
        rows = [(STEPS + side + r, cross[f, r]) for r in range(STEPS)]
        rows += [(2 * STEPS - side + r, chip[f, r]) for r in range(STEPS)]
        own[f] = pack(rows, blank)
    for f in range(fields):
        for g in range(fields):
            splat[f * fields + g] = jnp.full((8, LANES), mixing[f, g], jnp.float32)
    slabs[:, pl.ds(side, STEPS)] = cross[...]
    slabs[:, pl.ds(STEPS - side, STEPS)] = chip[...]
    for k in range(STEPS - 1):

        def tile(f, r):
            return made[k - 1, f, r] if k else slabs[f, r]

        def store(f, r, value):
            made[k, f, r] = value

        rows = list(range(k + 1, 2 * STEPS - k - 1))
        advance(splat, tile, lambda e, r: slabs[fields + e, r], rows, store)

    def products(f, totals):
        totals = list(totals)
        for x in range(2 * STEPS):
            old = [held[m, f, x] for m in range(STEPS)]
            for i, (a, b) in enumerate(PAIRS):
                totals[i] = totals[i] + old[a] * old[b]
        return tuple(totals)

    for i, total in enumerate(lax.fori_loop(0, fields, products, (blank,) * len(PAIRS))):
        old_sums[i] = total


def alone_kernel(splat, from_cross, cross, chip, from_chip, ahead, made, slabs, outer_rows):
    fields, rows = cross.shape[0] - EXTRA, 4 * STEPS
    side = STEPS * parity()
    for ref, row in (
        (from_cross, 3 * side),
        (cross, STEPS + side),
        (chip, 2 * STEPS - side),
        (from_chip, 3 * (STEPS - side)),
    ):
        slabs[:, pl.ds(row, STEPS)] = ref[...]

    def done(k, r):
        return STEPS + k < r < 3 * STEPS - k - 1

    for k in range(STEPS):

        def tile(f, r):
            if k == 0:
                return slabs[f, r]
            if STEPS <= r < 3 * STEPS:
                return (ahead if done(k - 1, r) else made)[k - 1, f, r - STEPS]
            return outer_rows[(k - 1) % 2, f, r if r < STEPS else r - 2 * STEPS]

        def put(f, r, value):
            if STEPS <= r < 3 * STEPS:
                made[k, f, r - STEPS] = value
            else:
                outer_rows[k % 2, f, r if r < STEPS else r - 2 * STEPS] = value

        left = [r for r in range(k + 1, rows - k - 1) if not done(k, r)]
        advance(splat, tile, lambda e, r: slabs[fields + e, r], left, put)


def krylov_kernel(
    splat, own, from_left, from_right, made, held, old_sums, krylov, sums, rim, change
):
    fields = held.shape[1]
    lane, wall = lane_index(), walls()
    place = lane % 8
    inner = place < 4
    for f in range(fields + EXTRA):
        mine, left, right = own[f], from_left[f // 2], from_right[f // 2]
        if f % 2:
            left, right = pltpu.roll(left, LANES - 4, 1), pltpu.roll(right, 4, 1)
        rim[0, f, 0] = jnp.where(inner, left, mine)
        rim[0, f, 1] = jnp.where(inner, mine, right)

    _, _, c_zu, c_zd = speeds(own[fields], own[fields + 1])
    c_zu, c_zd = jnp.where(place == 3, c_zu, 0.0), jnp.where(place == 4, c_zd, 0.0)
    for f in range(fields):
        change[0, f] = c_zu * pltpu.roll(rim[0, f, 1], LANES - 1, 1) + c_zd * pltpu.roll(rim[0, f, 0], 1, 1)

    for k in range(STEPS):

        def edge(e):
            values = [rim[k, f, e] for f in range(fields)]
            return (
                values,
                lambda f: pltpu.roll(values[f], LANES - 8, 1),
                lambda f: pltpu.roll(values[f], 8, 1),
                lambda f: pltpu.roll(values[f], LANES - 1, 1),
                lambda f: pltpu.roll(values[f], 1, 1),
                rim[0, fields, e],
                rim[0, fields + 1, e],
                rim[0, fields + 2, e],
            )

        def inside():
            values = [change[k - 1, f] for f in range(fields)]
            return (
                values,
                lambda f: pltpu.roll(values[f], LANES - 8, 1),
                lambda f: pltpu.roll(values[f], 8, 1),
                lambda f: pltpu.roll(jnp.where(place == 4, rim[k, f, 1], values[f]), LANES - 1, 1),
                lambda f: pltpu.roll(jnp.where(place == 3, rim[k, f, 0], values[f]), 1, 1),
                own[fields],
                own[fields + 1],
                own[fields + 2],
            )

        items = [edge(0), edge(1)] if k + 1 < STEPS else []
        edges = len(items)
        if k:
            items.append(inside())

        def store(i, f, value):
            if i < edges:
                rim[k + 1, f, i] = value
            else:
                change[k, f] = value

        stencil(splat, items, wall, store)

    face = (lane < STEPS) | (lane >= LANES - STEPS)

    def products(f, totals):
        totals = list(totals)
        for x in range(2 * STEPS):
            new = []
            for k in range(STEPS):
                turned = pltpu.roll(change[k, f], LANES - (8 * (x + STEPS) + 4), 1)
                new.append(made[k, f, x] + jnp.where(face, turned, 0.0))
                krylov[k, f, x] = new[k]
            old = [held[m, f, x] for m in range(STEPS)]
            i = 0
            for a in range(STEPS):
                for b in range(STEPS):
                    totals[i] = totals[i] + old[a] * new[b]
                    i += 1
            for a, b in PAIRS:
                totals[i] = totals[i] + new[a] * new[b]
                i += 1
        return tuple(totals)

    zero = jnp.zeros((8, LANES), jnp.float32)
    totals = (zero,) * (STEPS * STEPS + len(PAIRS))
    for f in range(fields):
        totals = products(f, totals)
    totals = list(totals) + [old_sums[i] for i in range(len(PAIRS))]
    lines = [jnp.sum(t, axis=0, keepdims=True) for t in totals]
    lines.append(jnp.zeros((LANES - len(lines), LANES), jnp.float32))
    table = jnp.concatenate(lines, axis=0)
    row_sums = lax.dot_general(
        jnp.ones((8, LANES), jnp.float32),
        table,
        (((1,), (1,)), ((), ())),
        precision=lax.Precision.HIGHEST,
        preferred_element_type=jnp.float32,
    )
    for i in range(sums.shape[0]):
        sums[i] = row_sums[0:1]


def finish_kernel(total, parts, krylov, basis, proj_out, factor_out, new_out):
    fields = basis.shape[1]
    line = parts[0]
    for i in range(1, parts.shape[0]):
        line = line + parts[i]
    line = jnp.broadcast_to(line / total, (8, LANES))
    spread = [
        jnp.broadcast_to(line[:, i : i + 1], (8, LANES))
        for i in range(STEPS * STEPS + 2 * len(PAIRS))
    ]
    proj = [[spread[a * STEPS + b] for b in range(STEPS)] for a in range(STEPS)]
    new_new, old_old = {}, {}
    for i, (a, b) in enumerate(PAIRS):
        new_new[a, b] = spread[STEPS * STEPS + i]
        old_old[a, b] = old_old[b, a] = spread[STEPS * STEPS + len(PAIRS) + i]
    turned = [
        [
            sum(old_old[j, i] * proj[i][k] for i in range(STEPS)) - 2.0 * proj[j][k]
            for k in range(STEPS)
        ]
        for j in range(STEPS)
    ]
    gram = {
        (a, b): new_new[a, b] + sum(proj[j][a] * turned[j][b] for j in range(STEPS))
        for a, b in PAIRS
    }
    lower, inverse = {}, []
    for b in range(STEPS):
        for a in range(b, STEPS):
            value = gram[b, a]
            for c in range(b):
                value = value - lower[a, c] * lower[b, c]
            if a == b:
                inverse.append(lax.rsqrt(value))
                lower[a, b] = value * inverse[b]
            else:
                lower[a, b] = value * inverse[b]
    lane, sub = lane_index(), row_index()
    proj_tile = jnp.zeros((8, LANES), jnp.float32)
    factor_tile = proj_tile
    for a in range(STEPS):
        for b in range(STEPS):
            here = (sub == a) & (lane == b)
            proj_tile = jnp.where(here, proj[a][b], proj_tile)
            if b >= a:
                factor_tile = jnp.where(here, lower[b, a], factor_tile)
    proj_out[...] = proj_tile[:STEPS, :STEPS]
    factor_out[...] = factor_tile[:STEPS, :STEPS]

    def field(f, carry):
        for x in range(2 * STEPS):
            old = [basis[m, f, x] for m in range(STEPS)]
            made = []
            for k in range(STEPS):
                value = krylov[k, f, x]
                for m in range(STEPS):
                    value = value - proj[m][k] * old[m]
                for c in range(k):
                    value = value - lower[k, c] * made[c]
                made.append(value * inverse[k])
                new_out[k, f, x] = made[k]
        return carry

    for f in range(fields):
        field(f, 0)


def far(*arrays):
    return [pltpu.with_memory_space_constraint(a, pltpu.HBM) for a in arrays]


def swaps(size, first):
    pairs = [(i, (i + 1) % size) for i in range(first, size, 2)]
    return pairs + [(j, i) for i, j in pairs]


def ring(axes, size):
    up = [(i, (i + 1) % size) for i in range(size)]
    down = [(j, i) for i, j in up]
    return lambda v: lax.ppermute(v, axes, up), lambda v: lax.ppermute(v, axes, down)


def shape_of(*dims):
    return jax.ShapeDtypeStruct(dims, jnp.float32)


def kept(*dims):
    return pltpu.VMEM(dims, jnp.float32)


def near(*arrays):
    return [pltpu.with_memory_space_constraint(a, pltpu.VMEM) for a in arrays]


def on_device(sizes, basis, coeffs, mixing_matrix, base_speed, span_speed, polymer_gain):
    outer, inner, span = sizes
    count, fields, nx, ny, nz = basis.shape
    total = float(basis[0].size * outer * inner * span)
    everything = fields + EXTRA
    slab = kept(everything, STEPS, ny, nz)
    vectors = (count, fields, nx, ny, nz)
    params = pltpu.CompilerParams(vmem_limit_bytes=16 * 2**20)
    cross, chip, held = pl.pallas_call(
        start_kernel,
        out_shape=(slab, slab, kept(*vectors)),
        in_specs=[HBM] * 5,
        out_specs=(VMEM,) * 3,
        scratch_shapes=[
            pltpu.SMEM((count,), jnp.float32),
            pltpu.SemaphoreType.DMA(()),
            pltpu.SemaphoreType.DMA((2, count)),
            pltpu.SemaphoreType.DMA((EXTRA, 2)),
        ],
        compiler_params=params,
        name="start",
    )(*far(coeffs, basis, base_speed, span_speed, polymer_gain))
    stream = ("outer", "inner")
    from_cross = lax.ppermute(cross, stream, swaps(outer * inner, 1))
    from_chip = lax.ppermute(chip, stream, swaps(outer * inner, 0))
    own, splat, old_sums, ahead = pl.pallas_call(
        prepare_kernel,
        out_shape=(
            kept(everything, ny, nz),
            kept(fields * fields, ny, nz),
            kept(len(PAIRS), ny, nz),
            kept(*vectors),
        ),
        in_specs=[SMEM] + [VMEM] * 3,
        out_specs=(VMEM,) * 4,
        scratch_shapes=[pltpu.VMEM((everything, 2 * STEPS, ny, nz), jnp.float32)],
        compiler_params=params,
        name="prepare",
    )(mixing_matrix, *near(cross, chip, held))
    halves = kept((everything + 1) // 2, ny, nz)
    packed, to_right, to_left = pl.pallas_call(
        edges_kernel,
        out_shape=(kept(everything, ny, nz), halves, halves),
        in_specs=[VMEM] * 3,
        out_specs=(VMEM,) * 3,
        compiler_params=params,
        name="edges",
    )(*near(from_cross, from_chip, own))
    up, down = ring("span", span)
    from_left, from_right = up(to_right), down(to_left)
    made = pl.pallas_call(
        alone_kernel,
        out_shape=kept(*vectors),
        in_specs=[VMEM] * 6,
        out_specs=VMEM,
        input_output_aliases={5: 0},
        scratch_shapes=[
            pltpu.VMEM((everything, 4 * STEPS, ny, nz), jnp.float32),
            pltpu.VMEM((2, fields, 2 * STEPS, ny, nz), jnp.float32),
        ],
        compiler_params=params,
        name="alone",
    )(*near(splat, from_cross, cross, chip, from_chip, ahead))
    krylov, sums = pl.pallas_call(
        krylov_kernel,
        out_shape=(kept(*vectors), kept(inner, 1, nz)),
        in_specs=[VMEM] * 7,
        out_specs=(VMEM,) * 2,
        scratch_shapes=[
            pltpu.VMEM((STEPS, everything, 2, ny, nz), jnp.float32),
            pltpu.VMEM((STEPS, fields, ny, nz), jnp.float32),
        ],
        compiler_params=params,
        name="krylov",
    )(*near(splat, packed, from_left, from_right, made, held, old_sums))
    sums = lax.all_to_all(sums, "inner", 0, 0, tiled=True)
    sums = jnp.broadcast_to(jnp.sum(sums, axis=0, keepdims=True), (outer * span, 1, nz))
    sums = lax.all_to_all(sums, ("outer", "span"), 0, 0, tiled=True)
    return pl.pallas_call(
        functools.partial(finish_kernel, total),
        out_shape=(shape_of(count, STEPS), shape_of(STEPS, STEPS), shape_of(*vectors)),
        in_specs=[VMEM] * 3,
        out_specs=(VMEM,) * 3,
        compiler_params=params,
        name="finish",
    )(*near(sums, krylov, held))


def solution(mesh):
    stream, span = mesh.shape["stream"], mesh.shape["span"]
    inner = 1
    while inner * inner < stream * span and stream % (2 * inner) == 0:
        inner *= 2
    outer = stream // inner
    split = Mesh(np.asarray(mesh.devices).reshape(outer, inner, span), ("outer", "inner", "span"))
    field = P(("outer", "inner"), None, "span")
    vectors = P(None, None, ("outer", "inner"), None, "span")
    return jax.shard_map(
        functools.partial(on_device, (outer, inner, span)),
        mesh=split,
        in_specs=(vectors, P(), P(), field, field, field),
        out_specs=(P(), P(), vectors),
        check_vma=False,
    )
```
